32 devices in a mesh: freq: 4 (over y, x), panel: 8 (over z, core).
Axes of the slice: x: 2, y: 2, z: 4, core: 2. Of those that a mesh axis runs over, the one named last changes fastest.
Arguments:
- fields: bfloat16 [128, 16, 16384], P('freq', None, 'panel'), may hold values from -6 to 6
- quad_index: int32 [16384], P('panel'), may hold values from 0 to 5
- band_width: int32 [128], P('freq'), may hold values from 1 to 64, as said below
Outputs:
- pair_blocks: float32 [128, 16384], P('freq', 'panel')
The draws below stay inside these ranges and needn't reach their ends.
Inputs may be any that keep to these rules, and one draw needn't show every extreme that they name: `band_width`: some frequency has band width exactly 64.
All inputs are finite; a program needn't handle non-finite values.
Results may differ from the reference program's by a relative error of at most 0.0029.
Values may be sent and summed in bfloat16 or wider, within the bound.
A program may use at most 128 MiB of HBM per device.

```python
import math
import jax
import jax.numpy as jnp
from jax import lax

COMP = 16
FREQS = 128
PANELS = 16384
BAND = 64


def draw_band_width(key, part):
    first_key, second_key = jax.random.split(key)
    widths = jax.random.randint(first_key, (FREQS,), 1, BAND + 1)
    widest = jax.random.randint(second_key, (), 0, FREQS)
    return jnp.where(jnp.arange(FREQS) == widest, BAND, widths).astype(jnp.int32)


def plant(values, rng, smallest, largest):
    longest = values.shape.index(max(values.shape))
    spots = []
    for shift in (0, 1):
        where = [jax.random.randint(jax.random.fold_in(rng, axis), (), 0, length) for axis, length in enumerate(values.shape)]
        where[longest] = (where[longest] + shift) % values.shape[longest]
        spots.append(tuple(where))
    return values.at[spots[0]].set(smallest).at[spots[1]].set(largest)


def level_of(rng, extent, cuts, least, high):
    factor_of = 1.0
    for dim, parts in cuts:
        draws = jax.random.uniform(jax.random.fold_in(jax.random.fold_in(rng, 6), dim), (parts,), jnp.float32, least / len(cuts), high / len(cuts))
        factor_of = factor_of * jnp.repeat(jnp.exp(draws), extent[dim] // parts).reshape((-1,) + (1,) * (len(extent) - 1 - dim))
    return factor_of


def bell_draw(key, extent, scale, bound, cuts=(), kind=jnp.bfloat16):
    entries = scale * jax.random.normal(key, extent, jnp.float32)
    if cuts:
        entries = entries * level_of(key, extent, cuts, -0.22, 0.18)
    return jnp.clip(entries, -bound, bound).astype(kind)


def setup_inputs(seed: int = 0) -> dict:
    keys = jax.random.split(jax.random.key(seed), 4)
    fields = bell_draw(keys[0], (FREQS, COMP, PANELS), 1.0, 6.0, ((0, 4), (2, 8)))
    quad_index = plant(jax.random.randint(keys[1], (PANELS,), 0, 6), jax.random.fold_in(keys[1], 1), 0, 5).astype(jnp.int32)
    band_width = draw_band_width(jax.random.fold_in(keys[3], 71), 0)
    return {"fields": fields, "quad_index": quad_index, "band_width": band_width}


QUAD_TABLE = (0.2, 0.45, 0.8, 1.1, 1.6, 2.3)

def reference(fields, quad_index, band_width):
    weight = jnp.asarray(QUAD_TABLE, jnp.float32)[quad_index]
    padded = jnp.concatenate([fields, jnp.zeros((BAND, COMP, PANELS), jnp.bfloat16)], 0)
    offsets = jnp.arange(BAND, dtype=jnp.int32) + 1

    def one_row(index):
        own = lax.dynamic_index_in_dim(fields, index, 0, keepdims=False)
        own_scaled = (own.astype(jnp.float32) * weight).astype(jnp.bfloat16)
        partner = lax.dynamic_slice_in_dim(padded, index + 1, BAND, 0).reshape(BAND * COMP, PANELS)
        gram = lax.dot_general(own_scaled, partner, (((1,), (1,)), ((), ())), preferred_element_type=jnp.float32)
        gram = gram.reshape(COMP, BAND, COMP).transpose(1, 0, 2)
        live = offsets <= band_width[index]
        return jnp.where(live[:, None, None], gram, jnp.float32(0.0)).reshape(BAND * COMP * COMP)
    rows = lax.map(one_row, jnp.arange(FREQS, dtype=jnp.int32))
    return rows * jnp.float32(1.0 / math.sqrt(PANELS))
```

```python
import functools
import math

import jax
import jax.numpy as jnp
from jax import lax
from jax.experimental import pallas as pl
from jax.experimental.pallas import tpu as pltpu
from jax.sharding import PartitionSpec as P

COMP = 16
REACH = 2
LANES = 128
CORES = 2
MESH = pl.DeviceIdType.MESH

QUAD_TABLE = (0.2, 0.45, 0.8, 1.1, 1.6, 2.3)


def shifted(x, axis, by):
    devices = lax.axis_size(axis)
    pairs = [(i, i + by) for i in range(devices) if 0 <= i + by < devices]
    return lax.ppermute(x, axis, pairs)


def plain(fields, quad_index, band_width):
    freq_local = fields.shape[0]
    panel_local = fields.shape[2]
    band = REACH * freq_local
    table = jnp.asarray(QUAD_TABLE, jnp.float32)
    matches = quad_index[None, :] == jnp.arange(6, dtype=jnp.int32)[:, None]
    weight = jnp.sum(jnp.where(matches, table[:, None], jnp.float32(0.0)), 0)
    scaled = (fields.astype(jnp.float32) * weight).astype(jnp.bfloat16)
    own_rows = scaled.reshape(freq_local * COMP, panel_local)
    partners = [fields]
    for distance in range(1, REACH + 1):
        partners.append(shifted(fields, "freq", -distance))
    grams = []
    for partner in partners:
        grams.append(
            lax.dot_general(
                own_rows,
                partner.reshape(freq_local * COMP, panel_local),
                (((1,), (1,)), ((), ())),
                preferred_element_type=jnp.float32,
            )
        )
    stacked = jnp.concatenate(grams, 1).reshape(freq_local, COMP, (REACH + 1) * freq_local, COMP)

    def pick_band(block, row_index):
        return lax.dynamic_slice_in_dim(block, row_index + 1, band, 1)

    picked = jax.vmap(pick_band)(stacked, jnp.arange(freq_local, dtype=jnp.int32))
    picked = picked.transpose(0, 2, 1, 3)
    offsets = jnp.arange(band, dtype=jnp.int32) + 1
    live_mask = offsets[None, :] <= band_width[:, None]
    picked = jnp.where(live_mask[:, :, None, None], picked, jnp.float32(0.0))
    panels_total = panel_local * lax.axis_size("panel")
    terms = picked.reshape(freq_local, band * COMP * COMP) * jnp.float32(
        1.0 / math.sqrt(panels_total)
    )
    return lax.psum_scatter(terms, "panel", scatter_dimension=1, tiled=True)


OWN, XG, DG = 0, 1, 2


def kernel(
    nf, npan, f_hbm, q_hbm, bw_hbm, out_ref,
    own, scaled, xbuf, ubuf, dbuf, xs, ds, acc, keep, away, cxin, zout, zin, total, give, fwd, fin,
    q_ref, bw_ref, near, local_sem, fsend, frecv, csend, crecv, zsend, zrecv, gsend, grecv,
):
    rows, panels = own.shape
    half = panels // 2
    block = rows
    freqs = rows // COMP
    oct_rows = 8 * COMP
    octs = rows // oct_rows
    nz = npan // CORES
    f32, bf16 = jnp.float32, jnp.bfloat16

    f = lax.axis_index("freq")
    p = lax.axis_index("panel")
    z, core = p // CORES, lax.rem(p, CORES)
    odd = lax.rem(f, 2)
    mate = f + 1 - 2 * odd
    has_u = f + 2 < nf
    has_d = f >= 2
    has_x = jnp.logical_or(odd == 1, has_u)
    partner = p + 1 - 2 * core

    def dev(ff, pp):
        return {"freq": ff, "panel": pp}


    barrier = pltpu.get_barrier_semaphore()
    below, above = z > 0, z < nz - 1

    def greet(ff, pp):
        pl.semaphore_signal(barrier, inc=1, device_id=dev(ff, pp), device_id_type=MESH)

    greet(mate, p)
    greet(f, partner)

    @pl.when(below)
    def _():
        greet(f, p - CORES)

    @pl.when(above)
    def _():
        greet(f, p + CORES)

    @pl.when(has_u)
    def _():
        greet(f + 2, p)

    @pl.when(has_d)
    def _():
        greet(f - 2, p)

    loads = [
        pltpu.make_async_copy(f_hbm, own, local_sem.at[0]),
        pltpu.make_async_copy(q_hbm, q_ref, local_sem.at[1]),
        pltpu.make_async_copy(bw_hbm, bw_ref, local_sem.at[2]),
    ]
    for load in loads:
        load.start()

    count = 2
    for there in (below, above, has_u, has_d):
        count = count + jnp.where(there, 1, 0)
    pl.semaphore_wait(barrier, count)

    def half_at(which):
        return pl.ds(pl.multiple_of(which * half, LANES), half)

    def rows_of(o, n=1):
        return pl.ds(pl.multiple_of(o * oct_rows, oct_rows), n * oct_rows)

    def field_copy(which, dst, slot, ff, o):
        return pltpu.make_async_remote_copy(
            src_ref=f_hbm.at[rows_of(o), half_at(which)], dst_ref=dst.at[rows_of(o), :],
            send_sem=fsend.at[slot, o], recv_sem=frecv.at[slot, o],
            device_id=dev(ff, p), device_id_type=MESH,
        )

    def to_mate(o):
        return field_copy(1 - odd, xbuf, 0, mate, o)

    def to_lower(o):
        return field_copy(0, ubuf, 1, f - 2, o)

    def to_upper(o):
        return field_copy(1, dbuf, 2, f + 2, o)

    for o in range(octs):
        to_mate(octs - 1 - o).start()

        @pl.when(has_d)
        def _(o=o):
            to_lower(o).start()

        @pl.when(has_u)
        def _(o=o):
            to_upper(octs - 1 - o).start()

    for far in range(1, nz - 1):
        @pl.when(jnp.logical_and(above, z >= far))
        def _(far=far):
            pl.semaphore_signal(near.at[0, far - 1], inc=1, device_id=dev(f, p + CORES), device_id_type=MESH)

        @pl.when(jnp.logical_and(below, z + far < nz))
        def _(far=far):
            pl.semaphore_signal(near.at[1, far - 1], inc=1, device_id=dev(f, p - CORES), device_id_type=MESH)

        @pl.when(z > far)
        def _(far=far):
            pl.semaphore_wait(near.at[0, far - 1], 1)

        @pl.when(z + 1 + far < nz)
        def _(far=far):
            pl.semaphore_wait(near.at[1, far - 1], 1)

    def weight_at(where):
        index = q_ref[:, where]
        w = jnp.zeros(index.shape, f32)
        for value, entry in enumerate(QUAD_TABLE):
            w = jnp.where(index == value, jnp.float32(entry), w)
        return w

    def scale(src, dst, where, o, n):
        w = weight_at(where)

        def step(i, carry):
            at = pl.ds(pl.multiple_of(o * oct_rows + i * 32, 32), 32)
            dst[at, :] = (src[at, :].astype(f32) * w).astype(bf16)
            return carry

        lax.fori_loop(0, n * oct_rows // 32, step, 0)

    def gram(left, left_at, lo, n, right, right_at, ro, m, slot, rel):
        tall = 2 if n % 2 == 0 else 1
        first_col = rel * block + ro * oct_rows

        def step(i, carry):
            at = rows_of(lo + i * tall, tall)
            acc[slot, at, first_col:first_col + m * oct_rows] = lax.dot_general(
                left[at, left_at], right[ro * oct_rows:(ro + m) * oct_rows, right_at],
                (((1,), (1,)), ((), ())), preferred_element_type=f32,
            )
            return carry

        if n == tall:
            step(0, 0)
        else:
            lax.fori_loop(0, n // tall, step, 0)

    def clear(slot, tile):
        acc[slot, :, tile * LANES:(tile + 1) * LANES] = jnp.zeros((rows, LANES), f32)

    clear(XG, octs - 1)
    clear(XG, 2 * octs)
    clear(DG, octs - 1)

    @pl.when(odd == 0)
    def _():
        clear(DG, 2 * octs - 1)

    @pl.when(odd == 1)
    def _():
        clear(OWN, octs)
        clear(OWN, 2 * octs - 1)

    @pl.when(jnp.logical_not(has_u))
    def _():
        clear(OWN, 2 * octs)

    def valid(slot, o, pp):
        t = o + pp
        low, high = t >= octs - 1, t <= 2 * octs - 1
        if slot == OWN:
            return jnp.logical_or(
                t <= octs - 1,
                jnp.logical_or(
                    jnp.logical_and(odd == 0, high),
                    jnp.logical_and(has_u, t >= 2 * octs - 1),
                ),
            )
        if slot == XG:
            return jnp.logical_and(has_x, jnp.logical_and(low, high))
        upper = jnp.logical_or(t >= 2 * octs - 1, jnp.logical_and(odd == 1, low))
        return jnp.logical_and(has_d, upper)

    def core_copy(slot, o, pp):
        zd = pp // CORES
        return pltpu.make_async_remote_copy(
            src_ref=away.at[slot, pp, rows_of(o), :], dst_ref=cxin.at[slot, zd, rows_of(o), :],
            send_sem=csend.at[slot, zd, o], recv_sem=crecv.at[slot, zd, o],
            device_id=dev(f, partner), device_id_type=MESH,
        )

    def z_copy(slot, o, zd, source):
        return pltpu.make_async_remote_copy(
            src_ref=zout.at[slot, zd, rows_of(o), :], dst_ref=zin.at[slot, source, rows_of(o), :],
            send_sem=zsend.at[slot, zd, o], recv_sem=zrecv.at[slot, source, o],
            device_id=dev(f, zd * CORES + core), device_id_type=MESH,
        )

    def walk(act, slot, o, t, n, do, dt):
        def step(i, carry):
            oo, tt = o + i * do, t + i * dt
            act(slot, oo, tt - oo, tt)
            return carry

        if n > 0:
            lax.fori_loop(0, n, step, 0)

    def make(slot, o, pp, t):
        lane = pl.multiple_of(t * LANES, LANES)
        for c in range(8):
            at = pl.ds(pl.multiple_of(o * oct_rows + c * COMP, COMP), COMP)
            if c == 7:
                value = acc[slot, at, pl.ds(pl.multiple_of(lane + LANES, LANES), LANES)]
            else:
                pair = acc[slot, at, pl.ds(lane, 2 * LANES)]
                value = pltpu.roll(pair, 2 * LANES - COMP * (c + 1), 1)[:, :LANES]
            keep[slot, pp, at, :] = value
            away[slot, pp, at, :] = value.astype(bf16)

        @pl.when(lax.rem(pp, CORES) != core)
        def _():
            core_copy(slot, o, pp).start()

    def join(slot, o, pp, t):
        @pl.when(lax.rem(pp, CORES) == core)
        def _():
            zd = pp // CORES
            core_copy(slot, o, pp).wait_recv()
            both = keep[slot, pp, rows_of(o), :] + cxin[slot, zd, rows_of(o), :].astype(f32)

            @pl.when(z == zd)
            def _():
                total[slot, rows_of(o), :] = both

            @pl.when(z != zd)
            def _():
                zout[slot, zd, rows_of(o), :] = both.astype(bf16)
                z_copy(slot, o, zd, z).start()

    def both_ways(jobs):
        for act in (make, join):
            for job in jobs:
                if len(job) == 2:
                    @pl.when(job[0])
                    def _(job=job, act=act):
                        for inner in job[1]:
                            walk(act, *inner)
                else:
                    walk(act, *job)

    for load in loads:
        load.wait()
    everything = pl.ds(0, panels)
    first = pl.ds(0, half)
    second = pl.ds(half, half)
    even_now, odd_now = odd == 0, odd == 1
    scale(own, scaled, everything, 0, octs)
    gram(scaled, everything, 0, octs, own, everything, 0, octs, OWN, 0)
    jobs = [(OWN, 0, t, t + 1, 1, 0) for t in range(octs - 1)]
    jobs.append((odd_now, [(OWN, 0, octs - 1, octs, 1, 0)]))
    both_ways(jobs)

    for i in range(octs):
        x = octs - 1 - i
        last = i == octs - 1
        to_mate(x).wait_recv()
        scale(xbuf, xs, half_at(odd), x, 1)
        jobs = []

        @pl.when(odd_now)
        def _(x=x):
            gram(xs, first, x, 1, own, second, 0, octs, XG, 1)

        jobs.append((odd_now, [(XG, x, octs - 1, octs + 1, 0, 1)]))

        @pl.when(even_now)
        def _(x=x):
            gram(scaled, first, 0, octs, xbuf, first, x, 1, OWN, 1)

        @pl.when(has_u)
        def _(i=i):
            to_lower(i).wait_recv()
            gram(scaled, first, i, octs - i, ubuf, first, i, 1, OWN, 2)

        @pl.when(jnp.logical_and(has_u, even_now))
        def _(i=i, x=x):
            gram(xs, first, x, 1, ubuf, first, 0, i + 1, XG, 1)
            if i:
                gram(xs, first, x + 1, i, ubuf, first, i, 1, XG, 1)

        mixed = [(XG, x, octs - 1, i + 1 + last, 0, 1), (XG, x + 1, octs - 1 + i, i, 1, 0)]
        if last:
            mixed.append((XG, x + 1, 2 * octs - 1, i, 1, 0))
        jobs.append((jnp.logical_and(has_u, even_now), mixed))

        @pl.when(has_d)
        def _(x=x):
            to_upper(x).wait_recv()
            scale(dbuf, ds, second, x, 1)
            gram(ds, first, x, 1, own, second, 0, x + 1, DG, 2)

        @pl.when(jnp.logical_and(has_d, odd_now))
        def _(i=i, x=x):
            gram(ds, first, x, 1, xbuf, first, x, i + 1, DG, 1)
            if i:
                gram(ds, first, x + 1, i, xbuf, first, x, 1, DG, 1)

        mixed = [
            (DG, x, octs + x - last, i + 1 + last, 0, 1),
            (DG, x + 1, octs + x, i, 1, 0),
            (DG, x, 2 * octs, x, 0, 1),
        ]
        if last:
            mixed.append((DG, x + 1, octs - 1, i, 1, 0))
        jobs.append((jnp.logical_and(has_d, odd_now), mixed))
        jobs.append((jnp.logical_and(has_d, even_now), [(DG, x, 2 * octs - 1, x + 1, 0, 1)]))
        own_even = [(OWN, 0, octs + x, octs, 1, 0)]
        if last:
            own_even.append((OWN, 0, octs - 1, octs, 1, 0))
        jobs.append((even_now, own_even))
        if i == 0:
            jobs.append((jnp.logical_and(has_u, odd_now), [(OWN, 0, 2 * octs - 1, octs, 1, 0)]))
        else:
            jobs.append((has_u, [(OWN, i, 2 * octs - 1 + i, octs - i, 1, 0)]))
        both_ways(jobs)

    def forward(slot, ff, o):
        return pltpu.make_async_remote_copy(
            src_ref=give.at[slot, rows_of(o), :], dst_ref=fwd.at[slot, rows_of(o), :],
            send_sem=gsend.at[slot, o], recv_sem=grecv.at[slot, o],
            device_id=dev(ff, p), device_id_type=MESH,
        )

    def settle(slot, target):
        def step(o, carry):
            here = valid(slot, o, p)

            @pl.when(here)
            def _():
                value = total[slot, rows_of(o), :]
                for hop in range(1, nz):
                    source = lax.rem(z + hop, nz)
                    z_copy(slot, o, z, source).wait_recv()
                    value = value + zin[slot, source, rows_of(o), :].astype(f32)
                total[slot, rows_of(o), :] = value
                if target is not None:
                    give[slot, rows_of(o), :] = value.astype(bf16)
                    forward(slot, target, o).start()

            if target is None:
                @pl.when(jnp.logical_not(here))
                def _():
                    total[slot, rows_of(o), :] = jnp.zeros((oct_rows, LANES), f32)

            return carry

        lax.fori_loop(0, octs, step, 0)

    settle(XG, mate)
    settle(DG, f - 2)
    settle(OWN, None)

    def drain(slot):
        def step(i, carry):
            pp, o = i // octs, lax.rem(i, octs)
            zd = pp // CORES

            @pl.when(valid(slot, o, pp))
            def _():
                @pl.when(lax.rem(pp, CORES) != core)
                def _():
                    core_copy(slot, o, pp).wait_send()

                @pl.when(jnp.logical_and(lax.rem(pp, CORES) == core, z != zd))
                def _():
                    z_copy(slot, o, zd, z).wait_send()

            return carry

        lax.fori_loop(0, npan * octs, step, 0)

    for slot in (OWN, XG, DG):
        drain(slot)

    mate_gives = jnp.logical_or(odd == 0, f + 1 < nf)

    def take(slot, giver, comes):
        def step(o, carry):
            @pl.when(comes(o))
            def _():
                forward(slot, giver, o).wait_recv()
                total[OWN, rows_of(o), :] = total[OWN, rows_of(o), :] + fwd[slot, rows_of(o), :].astype(f32)

            return carry

        lax.fori_loop(0, octs, step, 0)

    def from_mate(o):
        t = o + p
        return jnp.logical_and(mate_gives, jnp.logical_and(t >= octs - 1, t <= 2 * octs - 1))

    def from_upper(o):
        t = o + p
        reach = jnp.logical_or(t >= 2 * octs - 1, jnp.logical_and(odd == 1, t >= octs - 1))
        return jnp.logical_and(has_u, reach)

    take(XG, mate, from_mate)
    take(DG, f - 2, from_upper)

    fin[...] = total[OWN]
    eye = lax.broadcasted_iota(jnp.int32, (freqs, freqs), 0) == lax.broadcasted_iota(
        jnp.int32, (freqs, freqs), 1
    )
    width = jnp.sum(
        jnp.where(eye, jnp.broadcast_to(bw_ref[...].astype(f32), (freqs, freqs)), 0.0), 1, keepdims=True
    )
    width = jnp.broadcast_to(width, (freqs, LANES))
    norm = jnp.float32(1.0 / math.sqrt(panels * npan))
    part = lax.broadcasted_iota(jnp.int32, (freqs, LANES), 1) // COMP
    for h in range(COMP // 8):
        values = [fin[pl.ds(h * 8 + a, freqs, stride=COMP), :] for a in range(8)]
        for bit in (1, 2, 4):
            upper = lax.rem(part // bit, 2) == 1
            fresh = list(values)
            for i in range(8):
                if i & bit:
                    continue
                j = i | bit
                fresh[i] = jnp.where(upper, pltpu.roll(values[j], COMP * bit, 1), values[i])
                fresh[j] = jnp.where(upper, values[j], pltpu.roll(values[i], LANES - COMP * bit, 1))
            values = fresh
        for k in range(8):
            offset = (p * 8 + k + 1).astype(f32)
            live = offset <= width
            start = (k * (COMP // 8) + h) * LANES
            out_ref[:, start:start + LANES] = jnp.where(live, values[k] * norm, 0.0)

    def close(o, carry):
        to_mate(o).wait_send()

        @pl.when(has_d)
        def _():
            to_lower(o).wait_send()

        @pl.when(has_u)
        def _():
            to_upper(o).wait_send()

        @pl.when(valid(XG, o, p))
        def _():
            forward(XG, mate, o).wait_send()

        @pl.when(valid(DG, o, p))
        def _():
            forward(DG, f - 2, o).wait_send()

        return carry

    lax.fori_loop(0, octs, close, 0)


def fused(nf, npan, fields, quad_index, band_width):
    freqs, comp, panels = fields.shape
    rows = freqs * comp
    nz = npan // CORES
    half = panels // 2
    octs = freqs // 8
    out_cols = REACH * freqs * comp * comp // npan
    bf16, f32 = jnp.bfloat16, jnp.float32
    dma = pltpu.SemaphoreType.DMA
    vmem = pl.BlockSpec(memory_space=pltpu.VMEM)
    return pl.pallas_call(
        functools.partial(kernel, nf, npan),
        out_shape=jax.ShapeDtypeStruct((freqs, out_cols), f32),
        in_specs=[pl.BlockSpec(memory_space=pl.ANY)] * 3,
        out_specs=vmem,
        scratch_shapes=[
            pltpu.VMEM((rows, panels), bf16),
            pltpu.VMEM((rows, panels), bf16),
            pltpu.VMEM((rows, half), bf16),
            pltpu.VMEM((rows, half), bf16),
            pltpu.VMEM((rows, half), bf16),
            pltpu.VMEM((rows, half), bf16),
            pltpu.VMEM((rows, half), bf16),
            pltpu.VMEM((3, rows, (REACH + 1) * rows), f32),
            pltpu.VMEM((3, npan, rows, LANES), f32),
            pltpu.VMEM((3, npan, rows, LANES), bf16),
            pltpu.VMEM((3, nz, rows, LANES), bf16),
            pltpu.VMEM((3, nz, rows, LANES), bf16),
            pltpu.VMEM((3, nz, rows, LANES), bf16),
            pltpu.VMEM((3, rows, LANES), f32),
            pltpu.VMEM((3, rows, LANES), bf16),
            pltpu.VMEM((3, rows, LANES), bf16),
            pltpu.VMEM((rows, LANES), f32),
            pltpu.VMEM((1, panels), jnp.int32),
            pltpu.VMEM((1, freqs), jnp.int32),
            pltpu.SemaphoreType.REGULAR((2, max(nz - 2, 1))),
            dma((3,)),
            dma((3, octs)), dma((3, octs)),
            dma((3, nz, octs)), dma((3, nz, octs)),
            dma((3, nz, octs)), dma((3, nz, octs)),
            dma((3, octs)), dma((3, octs)),
        ],
        compiler_params=pltpu.CompilerParams(
            collective_id=0, has_side_effects=True, vmem_limit_bytes=58 * 1024 * 1024
        ),
    )(fields.reshape(rows, panels), quad_index.reshape(1, panels), band_width.reshape(1, freqs))


def local(nf, npan, fields, quad_index, band_width):
    freqs, comp, panels = fields.shape
    share = REACH * freqs * comp // npan
    fits = nf % 2 == 0 and npan % CORES == 0 and share == LANES and freqs % 8 == 0 and panels % (4 * LANES) == 0
    if not fits:
        return plain(fields, quad_index, band_width)
    return fused(nf, npan, fields, quad_index, band_width)


def solution(mesh):
    placed = (P("freq", None, "panel"), P("panel"), P("freq"))
    return jax.shard_map(
        functools.partial(local, mesh.shape["freq"], mesh.shape["panel"]),
        mesh=mesh, in_specs=placed, out_specs=P("freq", "panel"), check_vma=False,
    )
```

```python
import functools
import math

import jax
import jax.numpy as jnp
from jax import lax
from jax.experimental import pallas as pl
from jax.experimental.pallas import tpu as pltpu
from jax.sharding import PartitionSpec as P

COMP = 16
REACH = 2
LANES = 128
CORES = 2
MESH = pl.DeviceIdType.MESH

QUAD_TABLE = (0.2, 0.45, 0.8, 1.1, 1.6, 2.3)


def shifted(x, axis, by):
    devices = lax.axis_size(axis)
    pairs = [(i, i + by) for i in range(devices) if 0 <= i + by < devices]
    return lax.ppermute(x, axis, pairs)


def plain(fields, quad_index, band_width):
    freq_local = fields.shape[0]
    panel_local = fields.shape[2]
    band = REACH * freq_local
    table = jnp.asarray(QUAD_TABLE, jnp.float32)
    matches = quad_index[None, :] == jnp.arange(6, dtype=jnp.int32)[:, None]
    weight = jnp.sum(jnp.where(matches, table[:, None], jnp.float32(0.0)), 0)
    scaled = (fields.astype(jnp.float32) * weight).astype(jnp.bfloat16)
    own_rows = scaled.reshape(freq_local * COMP, panel_local)
    partners = [fields]
    for distance in range(1, REACH + 1):
        partners.append(shifted(fields, "freq", -distance))
    grams = []
    for partner in partners:
        grams.append(
            lax.dot_general(
                own_rows,
                partner.reshape(freq_local * COMP, panel_local),
                (((1,), (1,)), ((), ())),
                preferred_element_type=jnp.float32,
            )
        )
    stacked = jnp.concatenate(grams, 1).reshape(freq_local, COMP, (REACH + 1) * freq_local, COMP)

    def pick_band(block, row_index):
        return lax.dynamic_slice_in_dim(block, row_index + 1, band, 1)

    picked = jax.vmap(pick_band)(stacked, jnp.arange(freq_local, dtype=jnp.int32))
    picked = picked.transpose(0, 2, 1, 3)
    offsets = jnp.arange(band, dtype=jnp.int32) + 1
    live_mask = offsets[None, :] <= band_width[:, None]
    picked = jnp.where(live_mask[:, :, None, None], picked, jnp.float32(0.0))
    panels_total = panel_local * lax.axis_size("panel")
    terms = picked.reshape(freq_local, band * COMP * COMP) * jnp.float32(
        1.0 / math.sqrt(panels_total)
    )
    return lax.psum_scatter(terms, "panel", scatter_dimension=1, tiled=True)


OWN, XG, DG = 0, 1, 2


def pieces(octs, rising):
    rows = 8 * COMP
    found = [(o * rows, rows) for o in range(1, octs)]
    found = [(rows // 2, rows // 2), (0, rows // 2)] if not rising else []
    if rising:
        found = [(o * rows, rows) for o in range(octs - 1)]
        found += [((octs - 1) * rows, rows // 2), ((octs - 1) * rows + rows // 2, rows // 2)]
    else:
        found = [(o * rows, rows) for o in range(octs - 1, 0, -1)] + found
    return found


def arrival(octs, rising):
    unit = 4 * COMP
    when = {}
    for step, (start, rows) in enumerate(pieces(octs, rising)):
        for u in range(start // unit, (start + rows) // unit):
            when[u] = step
    return when


def ready(role, octs, x_at, y_at, slot, row, col):
    block, col = divmod(col, 2 * octs)
    even, low = role % 2 == 0, role < 2
    if slot == OWN:
        if block == 0:
            return 0
        if block == 1 and even:
            return 2 * x_at[col] + 2
        if block == 2 and low:
            return 2 * y_at[col] + 3
    if slot == XG and block == 1:
        if not even:
            return 2 * x_at[row] + 2
        if low:
            return 2 * max(x_at[row], y_at[col]) + 3
    if slot == DG and not low:
        if block == 2:
            return 2 * y_at[row] + 3
        if block == 1 and not even:
            return 2 * max(y_at[row], x_at[col]) + 3
    return None


def plan(role, octs, npan):
    x_at, y_at = arrival(octs, False), arrival(octs, role < 2)
    batches, blank = {}, set()
    for slot in (OWN, XG, DG):
        for o in range(octs):
            for pp in range(npan):
                t = o + pp
                halves = []
                for h in range(2):
                    times = [ready(role, octs, x_at, y_at, slot, 2 * o + h, 2 * t + h + k) for k in range(3)]
                    halves.append(times)
                if all(time is None for times in halves for time in times):
                    continue
                for h, times in enumerate(halves):
                    for k, time in enumerate(times):
                        if time is None:
                            blank.add((slot, (2 * t + h + k) // 2))
                due = [max([0] + [time for time in times if time is not None]) for times in halves]
                if due[0] == due[1]:
                    batches.setdefault(due[0], []).append((slot, o, 0, 2, pp))
                else:
                    for h in range(2):
                        batches.setdefault(due[h], []).append((slot, o, h, 1, pp))
    return batches, sorted(blank)


def kernel(
    nf, npan, f_hbm, q_hbm, bw_hbm, out_ref,
    own, scaled, xbuf, ybuf, xs, ys, acc, keep, away, cxin, zout, zin, total, give, fwd, fin,
    q_ref, bw_ref, near, local_sem, fsend, frecv, csend, crecv, zsend, zrecv, gsend, grecv,
):
    rows, panels = own.shape
    half = panels // 2
    block = rows
    freqs = rows // COMP
    oct_rows = 8 * COMP
    octs = rows // oct_rows
    nz = npan // CORES
    f32, bf16 = jnp.float32, jnp.bfloat16

    f = lax.axis_index("freq")
    p = lax.axis_index("panel")
    z, core = p // CORES, lax.rem(p, CORES)
    odd = lax.rem(f, 2)
    mate = f + 1 - 2 * odd
    has_u = f + 2 < nf
    has_d = f >= 2
    has_x = jnp.logical_or(odd == 1, has_u)
    partner = p + 1 - 2 * core

    def dev(ff, pp):
        return {"freq": ff, "panel": pp}


    barrier = pltpu.get_barrier_semaphore()
    below, above = z > 0, z < nz - 1

    def greet(ff, pp):
        pl.semaphore_signal(barrier, inc=1, device_id=dev(ff, pp), device_id_type=MESH)

    greet(mate, p)
    greet(f, partner)

    @pl.when(below)
    def _():
        greet(f, p - CORES)

    @pl.when(above)
    def _():
        greet(f, p + CORES)

    @pl.when(has_u)
    def _():
        greet(f + 2, p)

    @pl.when(has_d)
    def _():
        greet(f - 2, p)

    loads = [
        pltpu.make_async_copy(f_hbm, own, local_sem.at[0]),
        pltpu.make_async_copy(q_hbm, q_ref, local_sem.at[1]),
        pltpu.make_async_copy(bw_hbm, bw_ref, local_sem.at[2]),
    ]
    for load in loads:
        load.start()

    count = 2
    for there in (below, above, has_u, has_d):
        count = count + jnp.where(there, 1, 0)
    pl.semaphore_wait(barrier, count)

    def half_at(which):
        return pl.ds(pl.multiple_of(which * half, LANES), half)

    def rows_of(o, n=1):
        return pl.ds(pl.multiple_of(o * oct_rows, oct_rows), n * oct_rows)

    def field_copy(which, dst, slot, ff, step, rising):
        start, count = pieces(octs, rising)[step]
        return pltpu.make_async_remote_copy(
            src_ref=f_hbm.at[start:start + count, half_at(which)], dst_ref=dst.at[start:start + count, :],
            send_sem=fsend.at[slot, step], recv_sem=frecv.at[slot, step],
            device_id=dev(ff, p), device_id_type=MESH,
        )

    def to_mate(step):
        return field_copy(1 - odd, xbuf, 0, mate, step, False)

    def to_lower(step):
        return field_copy(0, ybuf, 1, f - 2, step, True)

    def to_upper(step):
        return field_copy(1, ybuf, 1, f + 2, step, False)

    steps = octs + 1
    for step in range(steps):
        to_mate(step).start()

        @pl.when(has_d)
        def _(step=step):
            to_lower(step).start()

        @pl.when(has_u)
        def _(step=step):
            to_upper(step).start()

    for far in range(1, nz - 1):
        @pl.when(jnp.logical_and(above, z >= far))
        def _(far=far):
            pl.semaphore_signal(near.at[0, far - 1], inc=1, device_id=dev(f, p + CORES), device_id_type=MESH)

        @pl.when(jnp.logical_and(below, z + far < nz))
        def _(far=far):
            pl.semaphore_signal(near.at[1, far - 1], inc=1, device_id=dev(f, p - CORES), device_id_type=MESH)

        @pl.when(z > far)
        def _(far=far):
            pl.semaphore_wait(near.at[0, far - 1], 1)

        @pl.when(z + 1 + far < nz)
        def _(far=far):
            pl.semaphore_wait(near.at[1, far - 1], 1)

    def weight_at(where):
        index = q_ref[:, where]
        w = jnp.zeros(index.shape, f32)
        for value, entry in enumerate(QUAD_TABLE):
            w = jnp.where(index == value, jnp.float32(entry), w)
        return w

    def scale(src, dst, where, start, count):
        w = weight_at(where)

        def step(i, carry):
            at = pl.ds(pl.multiple_of(start + i * 32, 32), 32)
            dst[at, :] = (src[at, :].astype(f32) * w).astype(bf16)
            return carry

        lax.fori_loop(0, count // 32, step, 0)

    def gram(left, left_at, lo, n, right, right_at, ro, m, slot, rel):
        tall = 256 if n % 256 == 0 else n
        first_col = rel * block + ro

        def step(i, carry):
            at = pl.ds(pl.multiple_of(lo + i * tall, 4 * COMP), tall)
            acc[slot, at, first_col:first_col + m] = lax.dot_general(
                left[at, left_at], right[ro:ro + m, right_at],
                (((1,), (1,)), ((), ())), preferred_element_type=f32,
            )
            return carry

        if n == tall:
            step(0, 0)
        else:
            lax.fori_loop(0, n // tall, step, 0)

    plans = [plan(role, octs, npan) for role in range(nf)]

    def each_role(act):
        for role in range(nf):
            @pl.when(f == role)
            def _(role=role):
                act(role)

    def clear(role):
        for slot, tile in plans[role][1]:
            acc[slot, :, tile * LANES:(tile + 1) * LANES] = jnp.zeros((rows, LANES), f32)

    each_role(clear)

    def valid(slot, o, pp):
        t = o + pp
        low, high = t >= octs - 1, t <= 2 * octs - 1
        if slot == OWN:
            return jnp.logical_or(
                t <= octs - 1,
                jnp.logical_or(
                    jnp.logical_and(odd == 0, high),
                    jnp.logical_and(has_u, t >= 2 * octs - 1),
                ),
            )
        if slot == XG:
            return jnp.logical_and(has_x, jnp.logical_and(low, high))
        upper = jnp.logical_or(t >= 2 * octs - 1, jnp.logical_and(odd == 1, low))
        return jnp.logical_and(has_d, upper)

    def span(o, h, n):
        return pl.ds((2 * o + h) * (oct_rows // 2), n * (oct_rows // 2))

    def core_copy(tile):
        slot, o, h, n, pp = tile
        zd = pp // CORES
        return pltpu.make_async_remote_copy(
            src_ref=away.at[slot, zd, span(o, h, n), :], dst_ref=cxin.at[slot, zd, span(o, h, n), :],
            send_sem=csend.at[slot, zd, 2 * o + h], recv_sem=crecv.at[slot, zd, 2 * o + h],
            device_id=dev(f, partner), device_id_type=MESH,
        )

    def z_copy(tile):
        slot, o, h, n, pp = tile
        zd = pp // CORES
        return pltpu.make_async_remote_copy(
            src_ref=zout.at[slot, zd, span(o, h, n), :], dst_ref=zin.at[slot, z, span(o, h, n), :],
            send_sem=zsend.at[slot, zd, 2 * o + h], recv_sem=zrecv.at[slot, z, o],
            device_id=dev(f, zd * CORES + core), device_id_type=MESH,
        )

    def from_z(slot, o, source):
        return pltpu.make_async_remote_copy(
            src_ref=zout.at[slot, z, rows_of(o), :], dst_ref=zin.at[slot, source, rows_of(o), :],
            send_sem=zsend.at[slot, z, 2 * o], recv_sem=zrecv.at[slot, source, o],
            device_id=dev(f, source * CORES + core), device_id_type=MESH,
        )

    def band(tile, put):
        slot, o, h, n, pp = tile
        lane = (o + pp) * LANES
        for c in range(4 * h, 4 * (h + n)):
            at = pl.ds(o * oct_rows + c * COMP, COMP)
            if c == 7:
                value = acc[slot, at, lane + LANES:lane + 2 * LANES]
            else:
                pair = acc[slot, at, lane:lane + 2 * LANES]
                value = pltpu.roll(pair, 2 * LANES - COMP * (c + 1), 1)[:, :LANES]
            put(at, value)

    def send(tile):
        slot, zd = tile[0], tile[4] // CORES

        def put(at, value):
            away[slot, zd, at, :] = value.astype(bf16)

        band(tile, put)
        core_copy(tile).start()

    def hold(tile):
        slot, zd = tile[0], tile[4] // CORES

        def put(at, value):
            keep[slot, zd, at, :] = value

        band(tile, put)

    def join(tile):
        slot, o, h, n, pp = tile
        zd = pp // CORES
        at = span(o, h, n)
        core_copy(tile).wait_recv()
        both = keep[slot, zd, at, :] + cxin[slot, zd, at, :].astype(f32)

        @pl.when(z == zd)
        def _():
            total[slot, at, :] = both

        @pl.when(z != zd)
        def _():
            zout[slot, zd, at, :] = both.astype(bf16)
            z_copy(tile).start()

    def sent(tile):
        core_copy(tile).wait_send()

    def joined(tile):
        @pl.when(z != tile[4] // CORES)
        def _():
            z_copy(tile).wait_send()

    def tiles(jobs):
        def run(role):
            for side in range(CORES):
                work = []
                for act, mine, batch in jobs:
                    for tile in plans[role][0].get(batch, []):
                        if (tile[4] % CORES == side) == mine:
                            work.append((act, tile))
                if work:
                    @pl.when(core == side)
                    def _(work=work):
                        for act, tile in work:
                            act(tile)

        each_role(run)

    def finish(*batches):
        tiles([(hold, True, b) for b in batches] + [(join, True, b) for b in batches])

    def drain(*batches):
        tiles([(sent, False, b) for b in batches] + [(joined, True, b) for b in batches])

    for load in loads:
        load.wait()
    everything = pl.ds(0, panels)
    first = pl.ds(0, half)
    second = pl.ds(half, half)
    even_now, odd_now = odd == 0, odd == 1
    scale(own, scaled, everything, 0, rows)
    gram(scaled, everything, 0, rows, own, everything, 0, rows, OWN, 0)
    tiles([(send, False, 0)])
    finish(0)

    for step in range(steps):
        x_from, x_rows = pieces(octs, False)[step]
        up_from, up_rows = pieces(octs, True)[step]
        x_end, up_end = x_from + x_rows, up_from + up_rows
        now, late = 2 * step + 2, 2 * step + 3
        drain(*((0,) if step == 0 else (now - 2, late - 2)))
        to_mate(step).wait_recv()

        @pl.when(odd_now)
        def _():
            scale(xbuf, xs, second, x_from, x_rows)
            gram(xs, first, x_from, x_rows, own, second, 0, rows, XG, 1)

        @pl.when(even_now)
        def _():
            gram(scaled, first, 0, rows, xbuf, first, x_from, x_rows, OWN, 1)

        tiles([(send, False, now)])

        @pl.when(has_u)
        def _():
            to_lower(step).wait_recv()
            gram(scaled, first, up_from, rows - up_from, ybuf, first, up_from, up_rows, OWN, 2)

        @pl.when(jnp.logical_and(has_u, even_now))
        def _():
            scale(xbuf, xs, first, x_from, x_rows)
            gram(xs, first, x_from, x_rows, ybuf, first, 0, up_end, XG, 1)
            if x_end < rows:
                gram(xs, first, x_end, rows - x_end, ybuf, first, up_from, up_rows, XG, 1)

        @pl.when(has_d)
        def _():
            to_upper(step).wait_recv()
            scale(ybuf, ys, second, x_from, x_rows)
            gram(ys, first, x_from, x_rows, own, second, 0, x_end, DG, 2)

        @pl.when(jnp.logical_and(has_d, odd_now))
        def _():
            gram(ys, first, x_from, x_rows, xbuf, first, x_from, rows - x_from, DG, 1)
            if x_end < rows:
                gram(ys, first, x_end, rows - x_end, xbuf, first, x_from, x_rows, DG, 1)

        tiles([(send, False, late)])
        finish(now, late)

    def forward(slot, ff, o):
        return pltpu.make_async_remote_copy(
            src_ref=give.at[slot, rows_of(o), :], dst_ref=fwd.at[slot, rows_of(o), :],
            send_sem=gsend.at[slot, o], recv_sem=grecv.at[slot, o],
            device_id=dev(ff, p), device_id_type=MESH,
        )

    def settle(slot, target):
        def step(o, carry):
            here = valid(slot, o, p)

            @pl.when(here)
            def _():
                value = total[slot, rows_of(o), :]
                for hop in range(1, nz):
                    source = lax.rem(z + hop, nz)
                    from_z(slot, o, source).wait_recv()
                    value = value + zin[slot, source, rows_of(o), :].astype(f32)
                total[slot, rows_of(o), :] = value
                if target is not None:
                    give[slot, rows_of(o), :] = value.astype(bf16)
                    forward(slot, target, o).start()

            if target is None:
                @pl.when(jnp.logical_not(here))
                def _():
                    total[slot, rows_of(o), :] = jnp.zeros((oct_rows, LANES), f32)

            return carry

        lax.fori_loop(0, octs, step, 0)

    settle(XG, mate)
    settle(DG, f - 2)
    settle(OWN, None)

    mate_gives = jnp.logical_or(odd == 0, f + 1 < nf)

    def take(slot, giver, comes):
        def step(o, carry):
            @pl.when(comes(o))
            def _():
                forward(slot, giver, o).wait_recv()
                total[OWN, rows_of(o), :] = total[OWN, rows_of(o), :] + fwd[slot, rows_of(o), :].astype(f32)

            return carry

        lax.fori_loop(0, octs, step, 0)

    def from_mate(o):
        t = o + p
        return jnp.logical_and(mate_gives, jnp.logical_and(t >= octs - 1, t <= 2 * octs - 1))

    def from_upper(o):
        t = o + p
        reach = jnp.logical_or(t >= 2 * octs - 1, jnp.logical_and(odd == 1, t >= octs - 1))
        return jnp.logical_and(has_u, reach)

    take(XG, mate, from_mate)
    take(DG, f - 2, from_upper)

    fin[...] = total[OWN]
    eye = lax.broadcasted_iota(jnp.int32, (freqs, freqs), 0) == lax.broadcasted_iota(
        jnp.int32, (freqs, freqs), 1
    )
    width = jnp.sum(
        jnp.where(eye, jnp.broadcast_to(bw_ref[...].astype(f32), (freqs, freqs)), 0.0), 1, keepdims=True
    )
    width = jnp.broadcast_to(width, (freqs, LANES))
    norm = jnp.float32(1.0 / math.sqrt(panels * npan))
    part = lax.broadcasted_iota(jnp.int32, (freqs, LANES), 1) // COMP
    for h in range(COMP // 8):
        values = [fin[pl.ds(h * 8 + a, freqs, stride=COMP), :] for a in range(8)]
        for bit in (1, 2, 4):
            upper = lax.rem(part // bit, 2) == 1
            fresh = list(values)
            for i in range(8):
                if i & bit:
                    continue
                j = i | bit
                fresh[i] = jnp.where(upper, pltpu.roll(values[j], COMP * bit, 1), values[i])
                fresh[j] = jnp.where(upper, values[j], pltpu.roll(values[i], LANES - COMP * bit, 1))
            values = fresh
        for k in range(8):
            offset = (p * 8 + k + 1).astype(f32)
            live = offset <= width
            start = (k * (COMP // 8) + h) * LANES
            out_ref[:, start:start + LANES] = jnp.where(live, values[k] * norm, 0.0)

    drain(2 * steps, 2 * steps + 1)
    for step in range(steps):
        to_mate(step).wait_send()

        @pl.when(has_d)
        def _(step=step):
            to_lower(step).wait_send()

        @pl.when(has_u)
        def _(step=step):
            to_upper(step).wait_send()

    def close(o, carry):
        @pl.when(valid(XG, o, p))
        def _():
            forward(XG, mate, o).wait_send()

        @pl.when(valid(DG, o, p))
        def _():
            forward(DG, f - 2, o).wait_send()

        return carry

    lax.fori_loop(0, octs, close, 0)


def fused(nf, npan, fields, quad_index, band_width):
    freqs, comp, panels = fields.shape
    rows = freqs * comp
    nz = npan // CORES
    half = panels // 2
    octs = freqs // 8
    out_cols = REACH * freqs * comp * comp // npan
    bf16, f32 = jnp.bfloat16, jnp.float32
    dma = pltpu.SemaphoreType.DMA
    vmem = pl.BlockSpec(memory_space=pltpu.VMEM)
    return pl.pallas_call(
        functools.partial(kernel, nf, npan),
        out_shape=jax.ShapeDtypeStruct((freqs, out_cols), f32),
        in_specs=[pl.BlockSpec(memory_space=pl.ANY)] * 3,
        out_specs=vmem,
        scratch_shapes=[
            pltpu.VMEM((rows, panels), bf16),
            pltpu.VMEM((rows, panels), bf16),
            pltpu.VMEM((rows, half), bf16),
            pltpu.VMEM((rows, half), bf16),
            pltpu.VMEM((rows, half), bf16),
            pltpu.VMEM((rows, half), bf16),
            pltpu.VMEM((3, rows, (REACH + 1) * rows), f32),
            pltpu.VMEM((3, nz, rows, LANES), f32),
            pltpu.VMEM((3, nz, rows, LANES), bf16),
            pltpu.VMEM((3, nz, rows, LANES), bf16),
            pltpu.VMEM((3, nz, rows, LANES), bf16),
            pltpu.VMEM((3, nz, rows, LANES), bf16),
            pltpu.VMEM((3, rows, LANES), f32),
            pltpu.VMEM((3, rows, LANES), bf16),
            pltpu.VMEM((3, rows, LANES), bf16),
            pltpu.VMEM((rows, LANES), f32),
            pltpu.VMEM((1, panels), jnp.int32),
            pltpu.VMEM((1, freqs), jnp.int32),
            pltpu.SemaphoreType.REGULAR((2, max(nz - 2, 1))),
            dma((3,)),
            dma((2, octs + 1)), dma((2, octs + 1)),
            dma((3, nz, 2 * octs)), dma((3, nz, 2 * octs)),
            dma((3, nz, 2 * octs)), dma((3, nz, octs)),
            dma((3, octs)), dma((3, octs)),
        ],
        compiler_params=pltpu.CompilerParams(
            collective_id=0, has_side_effects=True, vmem_limit_bytes=58 * 1024 * 1024
        ),
    )(fields.reshape(rows, panels), quad_index.reshape(1, panels), band_width.reshape(1, freqs))


def local(nf, npan, fields, quad_index, band_width):
    freqs, comp, panels = fields.shape
    share = REACH * freqs * comp // npan
    fits = nf == 2 * REACH and npan % CORES == 0 and share == LANES and freqs % 8 == 0 and panels % (4 * LANES) == 0
    if not fits:
        return plain(fields, quad_index, band_width)
    return fused(nf, npan, fields, quad_index, band_width)


def solution(mesh):
    placed = (P("freq", None, "panel"), P("panel"), P("freq"))
    return jax.shard_map(
        functools.partial(local, mesh.shape["freq"], mesh.shape["panel"]),
        mesh=mesh, in_specs=placed, out_specs=P("freq", "panel"), check_vma=False,
    )
```

```python
import functools
import math

import jax
import jax.numpy as jnp
from jax import lax
from jax.experimental import pallas as pl
from jax.experimental.pallas import tpu as pltpu
from jax.sharding import PartitionSpec as P

COMP = 16
REACH = 2
LANES = 128
CORES = 2
MESH = pl.DeviceIdType.MESH

QUAD_TABLE = (0.2, 0.45, 0.8, 1.1, 1.6, 2.3)


def shifted(x, axis, by):
    devices = lax.axis_size(axis)
    pairs = [(i, i + by) for i in range(devices) if 0 <= i + by < devices]
    return lax.ppermute(x, axis, pairs)


def plain(fields, quad_index, band_width):
    freq_local = fields.shape[0]
    panel_local = fields.shape[2]
    band = REACH * freq_local
    table = jnp.asarray(QUAD_TABLE, jnp.float32)
    matches = quad_index[None, :] == jnp.arange(6, dtype=jnp.int32)[:, None]
    weight = jnp.sum(jnp.where(matches, table[:, None], jnp.float32(0.0)), 0)
    scaled = (fields.astype(jnp.float32) * weight).astype(jnp.bfloat16)
    own_rows = scaled.reshape(freq_local * COMP, panel_local)
    partners = [fields]
    for distance in range(1, REACH + 1):
        partners.append(shifted(fields, "freq", -distance))
    grams = []
    for partner in partners:
        grams.append(
            lax.dot_general(
                own_rows,
                partner.reshape(freq_local * COMP, panel_local),
                (((1,), (1,)), ((), ())),
                preferred_element_type=jnp.float32,
            )
        )
    stacked = jnp.concatenate(grams, 1).reshape(freq_local, COMP, (REACH + 1) * freq_local, COMP)

    def pick_band(block, row_index):
        return lax.dynamic_slice_in_dim(block, row_index + 1, band, 1)

    picked = jax.vmap(pick_band)(stacked, jnp.arange(freq_local, dtype=jnp.int32))
    picked = picked.transpose(0, 2, 1, 3)
    offsets = jnp.arange(band, dtype=jnp.int32) + 1
    live_mask = offsets[None, :] <= band_width[:, None]
    picked = jnp.where(live_mask[:, :, None, None], picked, jnp.float32(0.0))
    panels_total = panel_local * lax.axis_size("panel")
    terms = picked.reshape(freq_local, band * COMP * COMP) * jnp.float32(
        1.0 / math.sqrt(panels_total)
    )
    return lax.psum_scatter(terms, "panel", scatter_dimension=1, tiled=True)


OWN, XG, DG = 0, 1, 2


def plan(role, octs, npan):
    even, low = role % 2 == 0, role < 2

    def due(slot, row, col):
        block, col = divmod(col, octs)
        x_row, x_col = octs - row, octs - col
        y_row, y_col = x_row, col + 1 if low else x_col
        if slot == OWN:
            if block == 0:
                return 0
            if block == 1 and even:
                return x_col
            if block == 2 and low:
                return y_col
        if slot == XG and block == 1:
            if not even:
                return x_row
            if low:
                return max(x_row, y_col)
        if slot == DG and not low:
            if block == 2:
                return y_row
            if block == 1 and not even:
                return max(y_row, x_col)
        return None

    batches = [[[] for _ in range(octs + 1)] for _ in range(CORES)]
    blank = set()
    for slot in (OWN, XG, DG):
        for o in range(octs):
            for pp in range(npan):
                t = o + pp
                times = [due(slot, o, t), due(slot, o, t + 1)]
                if times == [None, None]:
                    continue
                blank.update((slot, t + k) for k in range(2) if times[k] is None)
                last = max(time for time in times if time is not None)
                batches[pp % CORES][last].append((slot, o, pp // CORES))
    return batches, sorted(blank)


def kernel(
    nf, npan, f_hbm, q_hbm, bw_hbm, out_ref,
    own, scaled, xbuf, ybuf, xs, ys, acc, keep, away, cxin, zout, zin, total, give, fwd, fin,
    q_ref, bw_ref, near, local_sem, fsend, frecv, csend, crecv, zsend, zrecv, gsend, grecv,
):
    rows, panels = own.shape
    half = panels // 2
    block = rows
    freqs = rows // COMP
    oct_rows = 8 * COMP
    octs = rows // oct_rows
    nz = npan // CORES
    f32, bf16 = jnp.float32, jnp.bfloat16

    f = lax.axis_index("freq")
    p = lax.axis_index("panel")
    z, core = p // CORES, lax.rem(p, CORES)
    odd = lax.rem(f, 2)
    mate = f + 1 - 2 * odd
    has_u = f + 2 < nf
    has_d = f >= 2
    has_x = jnp.logical_or(odd == 1, has_u)
    partner = p + 1 - 2 * core

    def dev(ff, pp):
        return {"freq": ff, "panel": pp}


    barrier = pltpu.get_barrier_semaphore()
    below, above = z > 0, z < nz - 1

    def greet(ff, pp):
        pl.semaphore_signal(barrier, inc=1, device_id=dev(ff, pp), device_id_type=MESH)

    greet(mate, p)
    greet(f, partner)

    @pl.when(below)
    def _():
        greet(f, p - CORES)

    @pl.when(above)
    def _():
        greet(f, p + CORES)

    @pl.when(has_u)
    def _():
        greet(f + 2, p)

    @pl.when(has_d)
    def _():
        greet(f - 2, p)

    loads = [
        pltpu.make_async_copy(f_hbm, own, local_sem.at[0]),
        pltpu.make_async_copy(q_hbm, q_ref, local_sem.at[1]),
        pltpu.make_async_copy(bw_hbm, bw_ref, local_sem.at[2]),
    ]
    for load in loads:
        load.start()

    count = 2
    for there in (below, above, has_u, has_d):
        count = count + jnp.where(there, 1, 0)
    pl.semaphore_wait(barrier, count)

    def half_at(which):
        return pl.ds(pl.multiple_of(which * half, LANES), half)

    def rows_of(o, n=1):
        return pl.ds(pl.multiple_of(o * oct_rows, oct_rows), n * oct_rows)

    def field_copy(which, dst, slot, ff, step, o):
        return pltpu.make_async_remote_copy(
            src_ref=f_hbm.at[rows_of(o), half_at(which)], dst_ref=dst.at[rows_of(o), :],
            send_sem=fsend.at[slot, step], recv_sem=frecv.at[slot, step],
            device_id=dev(ff, p), device_id_type=MESH,
        )

    def to_mate(step):
        return field_copy(1 - odd, xbuf, 0, mate, step, octs - 1 - step)

    def to_lower(step):
        return field_copy(0, ybuf, 1, f - 2, step, step)

    def to_upper(step):
        return field_copy(1, ybuf, 1, f + 2, step, octs - 1 - step)

    def depart(step, carry):
        to_mate(step).start()

        @pl.when(has_d)
        def _():
            to_lower(step).start()

        @pl.when(has_u)
        def _():
            to_upper(step).start()

        return carry

    lax.fori_loop(0, octs, depart, 0)

    plans = [plan(role, octs, npan) for role in range(nf)]
    base = 1
    while base < 3 * octs * nz:
        base *= 2
    per = 1
    while base ** (per + 1) <= 2 ** 31:
        per += 1
    most = max(len(found) for lists, _ in plans for side in lists for found in side)
    words = max(-(-most // per), 1)

    def packed(found, w):
        value = 0
        for slot, o, zd in reversed(found[w * per:(w + 1) * per]):
            value = value * base + (slot * octs + o) * nz + zd
        return value

    def mine(seat, of):
        value = jnp.int32(0)
        for role in range(nf):
            for side in range(CORES):
                value = jnp.where(seat == role * CORES + side, jnp.int32(of(plans[role][0][side])), value)
        return value

    orders = []
    for seat in (f * CORES + 1 - core, f * CORES + core):
        orders.append([
            [mine(seat, lambda lists: len(lists[b]))]
            + [mine(seat, lambda lists: packed(lists[b], w)) for w in range(words)]
            for b in range(octs + 1)
        ])
    LEAVE, STAY = orders

    for far in range(1, nz - 1):
        @pl.when(jnp.logical_and(above, z >= far))
        def _(far=far):
            pl.semaphore_signal(near.at[0, far - 1], inc=1, device_id=dev(f, p + CORES), device_id_type=MESH)

        @pl.when(jnp.logical_and(below, z + far < nz))
        def _(far=far):
            pl.semaphore_signal(near.at[1, far - 1], inc=1, device_id=dev(f, p - CORES), device_id_type=MESH)

        @pl.when(z > far)
        def _(far=far):
            pl.semaphore_wait(near.at[0, far - 1], 1)

        @pl.when(z + 1 + far < nz)
        def _(far=far):
            pl.semaphore_wait(near.at[1, far - 1], 1)

    def weight_at(where):
        index = q_ref[:, where]
        w = jnp.zeros(index.shape, f32)
        for value, entry in enumerate(QUAD_TABLE):
            w = jnp.where(index == value, jnp.float32(entry), w)
        return w

    def scale(src, dst, where, start, count):
        w = weight_at(where)

        def step(i, carry):
            at = pl.ds(pl.multiple_of(start + i * 32, 32), 32)
            dst[at, :] = (src[at, :].astype(f32) * w).astype(bf16)
            return carry

        lax.fori_loop(0, count // 32, step, 0)

    def gram(left, left_at, lo, n, right, right_at, ro, m, slot, rel):
        tall = min(n, 256)
        cols = pl.ds(pl.multiple_of(rel * block + ro, LANES), m)
        over = pl.ds(ro, m)

        def step(i, carry):
            at = pl.ds(pl.multiple_of(lo + i * tall, oct_rows), tall)
            acc[slot, at, cols] = lax.dot_general(
                left[at, left_at], right[over, right_at],
                (((1,), (1,)), ((), ())), preferred_element_type=f32,
            )
            return carry

        if n == tall:
            step(0, 0)
        else:
            lax.fori_loop(0, n // tall, step, 0)

    for role in range(nf):
        @pl.when(f == role)
        def _(role=role):
            for slot, tile in plans[role][1]:
                acc[slot, :, tile * LANES:(tile + 1) * LANES] = jnp.zeros((rows, LANES), f32)

    def valid(slot, o, pp):
        t = o + pp
        low, high = t >= octs - 1, t <= 2 * octs - 1
        if slot == OWN:
            return jnp.logical_or(
                t <= octs - 1,
                jnp.logical_or(
                    jnp.logical_and(odd == 0, high),
                    jnp.logical_and(has_u, t >= 2 * octs - 1),
                ),
            )
        if slot == XG:
            return jnp.logical_and(has_x, jnp.logical_and(low, high))
        upper = jnp.logical_or(t >= 2 * octs - 1, jnp.logical_and(odd == 1, low))
        return jnp.logical_and(has_d, upper)

    def core_copy(slot, o, zd):
        return pltpu.make_async_remote_copy(
            src_ref=away.at[slot, zd, rows_of(o), :], dst_ref=cxin.at[slot, zd, rows_of(o), :],
            send_sem=csend.at[slot, zd, o], recv_sem=crecv.at[slot, zd, o],
            device_id=dev(f, partner), device_id_type=MESH,
        )

    def z_copy(slot, o, zd, source):
        return pltpu.make_async_remote_copy(
            src_ref=zout.at[slot, zd, rows_of(o), :], dst_ref=zin.at[slot, source, rows_of(o), :],
            send_sem=zsend.at[slot, zd, o], recv_sem=zrecv.at[slot, source, o],
            device_id=dev(f, zd * CORES + core), device_id_type=MESH,
        )

    def band(slot, o, zd, side, put):
        lane = pl.multiple_of((o + zd * CORES + side) * LANES, LANES)
        for c in range(8):
            at = pl.ds(pl.multiple_of(o * oct_rows + c * COMP, COMP), COMP)
            if c == 7:
                value = acc[slot, at, pl.ds(pl.multiple_of(lane + LANES, LANES), LANES)]
            else:
                pair = acc[slot, at, pl.ds(lane, 2 * LANES)]
                value = pltpu.roll(pair, 2 * LANES - COMP * (c + 1), 1)[:, :LANES]
            put(at, value)

    def send(slot, o, zd):
        def put(at, value):
            away[slot, zd, at, :] = value.astype(bf16)

        band(slot, o, zd, 1 - core, put)
        core_copy(slot, o, zd).start()

    def hold(slot, o, zd):
        def put(at, value):
            keep[slot, zd, at, :] = value

        band(slot, o, zd, core, put)

    def join(slot, o, zd):
        at = rows_of(o)
        core_copy(slot, o, zd).wait_recv()
        both = keep[slot, zd, at, :] + cxin[slot, zd, at, :].astype(f32)

        @pl.when(z == zd)
        def _():
            total[slot, at, :] = both

        @pl.when(z != zd)
        def _():
            zout[slot, zd, at, :] = both.astype(bf16)
            z_copy(slot, o, zd, z).start()

    def sent(slot, o, zd):
        core_copy(slot, o, zd).wait_send()

    def joined(slot, o, zd):
        @pl.when(z != zd)
        def _():
            z_copy(slot, o, zd, z).wait_send()

    def each(act, order, b):
        chosen = order[0]
        for bb in range(1, octs + 1):
            chosen = [jnp.where(b == bb, new, old) for new, old in zip(order[bb], chosen)]

        def step(k, carry):
            code = lax.rem(carry[0], base)
            carry = (lax.div(carry[0], base),) + carry[1:]
            fresh = lax.rem(k + 1, per) == 0
            carry = tuple(jnp.where(fresh, new, old) for new, old in zip(carry[1:] + carry[-1:], carry))
            act(lax.div(code, octs * nz), lax.rem(lax.div(code, nz), octs), lax.rem(code, nz))
            return carry

        lax.fori_loop(0, chosen[0], step, tuple(chosen[1:]))

    everything = pl.ds(0, panels)
    first = pl.ds(0, half)
    second = pl.ds(half, half)
    even_now, odd_now = odd == 0, odd == 1

    def batch(b, carry):
        @pl.when(b == 0)
        def _():
            for load in loads:
                load.wait()
            scale(own, scaled, everything, 0, rows)
            gram(scaled, everything, 0, rows, own, everything, 0, rows, OWN, 0)

        @pl.when(b > 0)
        def _():
            step = b - 1
            down = pl.multiple_of((octs - 1 - step) * oct_rows, oct_rows)
            up = pl.multiple_of(step * oct_rows, oct_rows)
            to_mate(step).wait_recv()

            @pl.when(odd_now)
            def _():
                scale(xbuf, xs, second, down, oct_rows)
                gram(xs, first, down, oct_rows, own, second, 0, rows, XG, 1)

            @pl.when(even_now)
            def _():
                gram(scaled, first, 0, rows, xbuf, first, down, oct_rows, OWN, 1)

            @pl.when(has_u)
            def _():
                to_lower(step).wait_recv()
                gram(scaled, first, 0, rows, ybuf, first, up, oct_rows, OWN, 2)

            @pl.when(jnp.logical_and(has_u, even_now))
            def _():
                scale(xbuf, xs, first, down, oct_rows)

                def cross(j, carry):
                    gram(xs, first, down, oct_rows, ybuf, first, pl.multiple_of(j * oct_rows, oct_rows), oct_rows, XG, 1)
                    gram(xs, first, pl.multiple_of((octs - 1 - j) * oct_rows, oct_rows), oct_rows, ybuf, first, up, oct_rows, XG, 1)
                    return carry

                lax.fori_loop(0, b, cross, 0)

            @pl.when(has_d)
            def _():
                to_upper(step).wait_recv()
                scale(ybuf, ys, second, down, oct_rows)
                gram(ys, first, down, oct_rows, own, second, 0, rows, DG, 2)

            @pl.when(jnp.logical_and(has_d, odd_now))
            def _():
                def cross(j, carry):
                    there = pl.multiple_of((octs - 1 - j) * oct_rows, oct_rows)
                    gram(ys, first, down, oct_rows, xbuf, first, there, oct_rows, DG, 1)
                    gram(ys, first, there, oct_rows, xbuf, first, down, oct_rows, DG, 1)
                    return carry

                lax.fori_loop(0, b, cross, 0)

        each(send, LEAVE, b)
        each(hold, STAY, b)
        each(join, STAY, b)
        return carry

    lax.fori_loop(0, octs + 1, batch, 0)

    def drain(b, carry):
        each(sent, LEAVE, b)
        each(joined, STAY, b)
        return carry

    lax.fori_loop(0, octs, drain, 0)

    def forward(slot, ff, o):
        return pltpu.make_async_remote_copy(
            src_ref=give.at[slot, rows_of(o), :], dst_ref=fwd.at[slot, rows_of(o), :],
            send_sem=gsend.at[slot, o], recv_sem=grecv.at[slot, o],
            device_id=dev(ff, p), device_id_type=MESH,
        )

    def settle(slot, target):
        def step(o, carry):
            here = valid(slot, o, p)

            @pl.when(here)
            def _():
                value = total[slot, rows_of(o), :]
                for hop in range(1, nz):
                    source = lax.rem(z + hop, nz)
                    z_copy(slot, o, z, source).wait_recv()
                    value = value + zin[slot, source, rows_of(o), :].astype(f32)
                total[slot, rows_of(o), :] = value
                if target is not None:
                    give[slot, rows_of(o), :] = value.astype(bf16)
                    forward(slot, target, o).start()

            if target is None:
                @pl.when(jnp.logical_not(here))
                def _():
                    total[slot, rows_of(o), :] = jnp.zeros((oct_rows, LANES), f32)

            return carry

        lax.fori_loop(0, octs, step, 0)

    settle(XG, mate)
    settle(DG, f - 2)
    settle(OWN, None)

    mate_gives = jnp.logical_or(odd == 0, f + 1 < nf)

    def take(slot, giver, comes):
        def step(o, carry):
            @pl.when(comes(o))
            def _():
                forward(slot, giver, o).wait_recv()
                total[OWN, rows_of(o), :] = total[OWN, rows_of(o), :] + fwd[slot, rows_of(o), :].astype(f32)

            return carry

        lax.fori_loop(0, octs, step, 0)

    def from_mate(o):
        t = o + p
        return jnp.logical_and(mate_gives, jnp.logical_and(t >= octs - 1, t <= 2 * octs - 1))

    def from_upper(o):
        t = o + p
        reach = jnp.logical_or(t >= 2 * octs - 1, jnp.logical_and(odd == 1, t >= octs - 1))
        return jnp.logical_and(has_u, reach)

    take(XG, mate, from_mate)
    take(DG, f - 2, from_upper)

    fin[...] = total[OWN]
    eye = lax.broadcasted_iota(jnp.int32, (freqs, freqs), 0) == lax.broadcasted_iota(
        jnp.int32, (freqs, freqs), 1
    )
    width = jnp.sum(
        jnp.where(eye, jnp.broadcast_to(bw_ref[...].astype(f32), (freqs, freqs)), 0.0), 1, keepdims=True
    )
    width = jnp.broadcast_to(width, (freqs, LANES))
    norm = jnp.float32(1.0 / math.sqrt(panels * npan))
    part = lax.broadcasted_iota(jnp.int32, (freqs, LANES), 1) // COMP
    for h in range(COMP // 8):
        values = [fin[pl.ds(h * 8 + a, freqs, stride=COMP), :] for a in range(8)]
        for bit in (1, 2, 4):
            upper = lax.rem(part // bit, 2) == 1
            fresh = list(values)
            for i in range(8):
                if i & bit:
                    continue
                j = i | bit
                fresh[i] = jnp.where(upper, pltpu.roll(values[j], COMP * bit, 1), values[i])
                fresh[j] = jnp.where(upper, values[j], pltpu.roll(values[i], LANES - COMP * bit, 1))
            values = fresh
        for k in range(8):
            offset = (p * 8 + k + 1).astype(f32)
            live = offset <= width
            start = (k * (COMP // 8) + h) * LANES
            out_ref[:, start:start + LANES] = jnp.where(live, values[k] * norm, 0.0)

    drain(octs, 0)

    def close(o, carry):
        to_mate(o).wait_send()

        @pl.when(has_d)
        def _():
            to_lower(o).wait_send()

        @pl.when(has_u)
        def _():
            to_upper(o).wait_send()

        @pl.when(valid(XG, o, p))
        def _():
            forward(XG, mate, o).wait_send()

        @pl.when(valid(DG, o, p))
        def _():
            forward(DG, f - 2, o).wait_send()

        return carry

    lax.fori_loop(0, octs, close, 0)


def fused(nf, npan, fields, quad_index, band_width):
    freqs, comp, panels = fields.shape
    rows = freqs * comp
    nz = npan // CORES
    half = panels // 2
    octs = freqs // 8
    out_cols = REACH * freqs * comp * comp // npan
    bf16, f32 = jnp.bfloat16, jnp.float32
    dma = pltpu.SemaphoreType.DMA
    vmem = pl.BlockSpec(memory_space=pltpu.VMEM)
    return pl.pallas_call(
        functools.partial(kernel, nf, npan),
        out_shape=jax.ShapeDtypeStruct((freqs, out_cols), f32),
        in_specs=[pl.BlockSpec(memory_space=pl.ANY)] * 3,
        out_specs=vmem,
        scratch_shapes=[
            pltpu.VMEM((rows, panels), bf16),
            pltpu.VMEM((rows, panels), bf16),
            pltpu.VMEM((rows, half), bf16),
            pltpu.VMEM((rows, half), bf16),
            pltpu.VMEM((rows, half), bf16),
            pltpu.VMEM((rows, half), bf16),
            pltpu.VMEM((3, rows, (REACH + 1) * rows), f32),
            pltpu.VMEM((3, nz, rows, LANES), f32),
            pltpu.VMEM((3, nz, rows, LANES), bf16),
            pltpu.VMEM((3, nz, rows, LANES), bf16),
            pltpu.VMEM((3, nz, rows, LANES), bf16),
            pltpu.VMEM((3, nz, rows, LANES), bf16),
            pltpu.VMEM((3, rows, LANES), f32),
            pltpu.VMEM((3, rows, LANES), bf16),
            pltpu.VMEM((3, rows, LANES), bf16),
            pltpu.VMEM((rows, LANES), f32),
            pltpu.VMEM((1, panels), jnp.int32),
            pltpu.VMEM((1, freqs), jnp.int32),
            pltpu.SemaphoreType.REGULAR((2, max(nz - 2, 1))),
            dma((3,)),
            dma((2, octs)), dma((2, octs)),
            dma((3, nz, octs)), dma((3, nz, octs)),
            dma((3, nz, octs)), dma((3, nz, octs)),
            dma((3, octs)), dma((3, octs)),
        ],
        compiler_params=pltpu.CompilerParams(
            collective_id=0, has_side_effects=True, vmem_limit_bytes=58 * 1024 * 1024
        ),
    )(fields.reshape(rows, panels), quad_index.reshape(1, panels), band_width.reshape(1, freqs))


def local(nf, npan, fields, quad_index, band_width):
    freqs, comp, panels = fields.shape
    share = REACH * freqs * comp // npan
    fits = nf == 2 * REACH and npan % CORES == 0 and share == LANES and freqs % 8 == 0 and panels % (4 * LANES) == 0
    if not fits:
        return plain(fields, quad_index, band_width)
    return fused(nf, npan, fields, quad_index, band_width)


def solution(mesh):
    placed = (P("freq", None, "panel"), P("panel"), P("freq"))
    return jax.shard_map(
        functools.partial(local, mesh.shape["freq"], mesh.shape["panel"]),
        mesh=mesh, in_specs=placed, out_specs=P("freq", "panel"), check_vma=False,
    )
```

```python
import functools
import math

import jax
import jax.numpy as jnp
from jax import lax
from jax.experimental import pallas as pl
from jax.experimental.pallas import tpu as pltpu
from jax.sharding import PartitionSpec as P

COMP = 16
REACH = 2
LANES = 128
CORES = 2
MESH = pl.DeviceIdType.MESH

QUAD_TABLE = (0.2, 0.45, 0.8, 1.1, 1.6, 2.3)


def shifted(x, axis, by):
    devices = lax.axis_size(axis)
    pairs = [(i, i + by) for i in range(devices) if 0 <= i + by < devices]
    return lax.ppermute(x, axis, pairs)


def plain(fields, quad_index, band_width):
    freq_local = fields.shape[0]
    panel_local = fields.shape[2]
    band = REACH * freq_local
    table = jnp.asarray(QUAD_TABLE, jnp.float32)
    matches = quad_index[None, :] == jnp.arange(6, dtype=jnp.int32)[:, None]
    weight = jnp.sum(jnp.where(matches, table[:, None], jnp.float32(0.0)), 0)
    scaled = (fields.astype(jnp.float32) * weight).astype(jnp.bfloat16)
    own_rows = scaled.reshape(freq_local * COMP, panel_local)
    partners = [fields]
    for distance in range(1, REACH + 1):
        partners.append(shifted(fields, "freq", -distance))
    grams = []
    for partner in partners:
        grams.append(
            lax.dot_general(
                own_rows,
                partner.reshape(freq_local * COMP, panel_local),
                (((1,), (1,)), ((), ())),
                preferred_element_type=jnp.float32,
            )
        )
    stacked = jnp.concatenate(grams, 1).reshape(freq_local, COMP, (REACH + 1) * freq_local, COMP)

    def pick_band(block, row_index):
        return lax.dynamic_slice_in_dim(block, row_index + 1, band, 1)

    picked = jax.vmap(pick_band)(stacked, jnp.arange(freq_local, dtype=jnp.int32))
    picked = picked.transpose(0, 2, 1, 3)
    offsets = jnp.arange(band, dtype=jnp.int32) + 1
    live_mask = offsets[None, :] <= band_width[:, None]
    picked = jnp.where(live_mask[:, :, None, None], picked, jnp.float32(0.0))
    panels_total = panel_local * lax.axis_size("panel")
    terms = picked.reshape(freq_local, band * COMP * COMP) * jnp.float32(
        1.0 / math.sqrt(panels_total)
    )
    return lax.psum_scatter(terms, "panel", scatter_dimension=1, tiled=True)


OWN, XG, DG = 0, 1, 2


def plan(role, octs, npan):
    even, low = role % 2 == 0, role < 2

    def due(slot, row, col):
        block, col = divmod(col, octs)
        x_row, x_col = octs - row, octs - col
        y_row, y_col = x_row, col + 1 if low else x_col
        if slot == OWN:
            if block == 0:
                return 0
            if block == 1 and even:
                return x_col
            if block == 2 and low:
                return y_col
        if slot == XG and block == 1:
            if not even:
                return x_row
            if low:
                return max(x_row, y_col)
        if slot == DG and not low:
            if block == 2:
                return y_row
            if block == 1 and not even:
                return max(y_row, x_col)
        return None

    batches = [[[] for _ in range(octs + 1)] for _ in range(CORES)]
    blank = set()
    for slot in (XG, DG, OWN):
        for o in range(octs):
            for pp in range(npan):
                t = o + pp
                times = [due(slot, o, t), due(slot, o, t + 1)]
                if times == [None, None]:
                    continue
                blank.update((slot, t + k) for k in range(2) if times[k] is None)
                last = max(time for time in times if time is not None)
                batches[pp % CORES][last].append((slot, o, pp // CORES))
    return batches, sorted(blank)


def kernel(
    nf, npan, f_hbm, q_hbm, bw_hbm, out_ref,
    own, scaled, xbuf, ybuf, xs, ys, acc, keep, away, cxin, zout, zin, total, give, fwd, fin, relay, direct,
    q_ref, bw_ref, near, local_sem, fsend, frecv, csend, crecv, zsend, zrecv, gsend, grecv, rsend, rrecv, drecv,
):
    rows, panels = own.shape
    half = panels // 2
    block = rows
    freqs = rows // COMP
    oct_rows = 8 * COMP
    octs = rows // oct_rows
    nz = npan // CORES
    f32, bf16 = jnp.float32, jnp.bfloat16

    f = lax.axis_index("freq")
    p = lax.axis_index("panel")
    z, core = p // CORES, lax.rem(p, CORES)
    odd = lax.rem(f, 2)
    mate = f + 1 - 2 * odd
    has_u = f + 2 < nf
    has_d = f >= 2
    has_x = jnp.logical_or(odd == 1, has_u)
    partner = p + 1 - 2 * core

    def dev(ff, pp):
        return {"freq": ff, "panel": pp}


    barrier = pltpu.get_barrier_semaphore()
    below, above = z > 0, z < nz - 1

    def greet(ff, pp):
        pl.semaphore_signal(barrier, inc=1, device_id=dev(ff, pp), device_id_type=MESH)

    greet(mate, p)
    greet(f, partner)

    @pl.when(below)
    def _():
        greet(f, p - CORES)

    @pl.when(above)
    def _():
        greet(f, p + CORES)

    @pl.when(has_u)
    def _():
        greet(f + 2, p)

    @pl.when(has_d)
    def _():
        greet(f - 2, p)

    loads = [
        pltpu.make_async_copy(f_hbm, own, local_sem.at[0]),
        pltpu.make_async_copy(q_hbm, q_ref, local_sem.at[1]),
        pltpu.make_async_copy(bw_hbm, bw_ref, local_sem.at[2]),
    ]
    for load in loads:
        load.start()

    count = 2
    for there in (below, above, has_u, has_d):
        count = count + jnp.where(there, 1, 0)
    pl.semaphore_wait(barrier, count)

    def half_at(which):
        return pl.ds(pl.multiple_of(which * half, LANES), half)

    def rows_of(o, n=1):
        return pl.ds(pl.multiple_of(o * oct_rows, oct_rows), n * oct_rows)

    def field_copy(which, dst, slot, ff, step, o):
        return pltpu.make_async_remote_copy(
            src_ref=f_hbm.at[rows_of(o), half_at(which)], dst_ref=dst.at[rows_of(o), :],
            send_sem=fsend.at[slot, step], recv_sem=frecv.at[slot, step],
            device_id=dev(ff, p), device_id_type=MESH,
        )

    def to_mate(step):
        return field_copy(1 - odd, xbuf, 0, mate, step, octs - 1 - step)

    def to_lower(step):
        return field_copy(0, ybuf, 1, f - 2, step, step)

    def to_upper(step):
        return field_copy(1, ybuf, 1, f + 2, step, octs - 1 - step)

    def depart(step, carry):
        to_mate(step).start()

        @pl.when(has_d)
        def _():
            to_lower(step).start()

        @pl.when(has_u)
        def _():
            to_upper(step).start()

        return carry

    lax.fori_loop(0, octs, depart, 0)

    plans = [plan(role, octs, npan) for role in range(nf)]
    base = 1
    while base < 3 * octs * nz:
        base *= 2
    per = 1
    while base ** (per + 1) <= 2 ** 31:
        per += 1
    most = max(len(found) for lists, _ in plans for side in lists for found in side)
    words = max(-(-most // per), 1)

    def packed(found, w):
        value = 0
        for slot, o, zd in reversed(found[w * per:(w + 1) * per]):
            value = value * base + (slot * octs + o) * nz + zd
        return value

    def mine(seat, of):
        value = jnp.int32(0)
        for role in range(nf):
            for side in range(CORES):
                value = jnp.where(seat == role * CORES + side, jnp.int32(of(role, side)), value)
        return value

    orders = []
    for seat in (f * CORES + 1 - core, f * CORES + core):
        orders.append([
            [mine(seat, lambda role, side: len(plans[role][0][side][b]))]
            + [mine(seat, lambda role, side: packed(plans[role][0][side][b], w)) for w in range(words)]
            for b in range(octs + 1)
        ])
    LEAVE, STAY = orders
    busy = jnp.logical_or(jnp.logical_and(has_u, odd == 0), jnp.logical_and(has_d, odd == 1))

    def crossing(role, side):
        busy = (role < 2) == (role % 2 == 0)
        return [tile for tile in plans[role][0][side][octs] if busy and tile[0] == XG]

    passing = [mine(mate * CORES + core, lambda role, side: len(crossing(role, side)))]
    passing += [mine(mate * CORES + core, lambda role, side: packed(crossing(role, side), w)) for w in range(words)]

    def tell(far):
        @pl.when(jnp.logical_and(above, z >= far))
        def _():
            pl.semaphore_signal(near.at[0, far - 1], inc=1, device_id=dev(f, p + CORES), device_id_type=MESH)

        @pl.when(jnp.logical_and(below, z + far < nz))
        def _():
            pl.semaphore_signal(near.at[1, far - 1], inc=1, device_id=dev(f, p - CORES), device_id_type=MESH)

    def hear(far):
        @pl.when(z > far)
        def _():
            pl.semaphore_wait(near.at[0, far - 1], 1)

        @pl.when(z + 1 + far < nz)
        def _():
            pl.semaphore_wait(near.at[1, far - 1], 1)

    def late_bits(giver):
        value = jnp.int32(0)
        for role in range(nf):
            for pp in range(npan):
                bits = sum(2 ** o for _, o, zd in crossing(role, pp % CORES) if zd == pp // CORES)
                if bits:
                    value = jnp.where(jnp.logical_and(giver == role, p == pp), jnp.int32(bits), value)
        return value

    def is_late(bits, o):
        picked = jnp.int32(0)
        for oo in range(octs):
            picked = jnp.where(o == oo, lax.rem(lax.div(bits, 2 ** oo), 2), picked)
        return picked == 1

    given = late_bits(f)
    got = late_bits(mate)
    tell(1)

    def weight_at(where):
        index = q_ref[:, where]
        w = jnp.zeros(index.shape, f32)
        for value, entry in enumerate(QUAD_TABLE):
            w = jnp.where(index == value, jnp.float32(entry), w)
        return w

    def scale(src, dst, where, start, count):
        w = weight_at(where)

        def step(i, carry):
            at = pl.ds(pl.multiple_of(start + i * 32, 32), 32)
            dst[at, :] = (src[at, :].astype(f32) * w).astype(bf16)
            return carry

        lax.fori_loop(0, count // 32, step, 0)

    def gram(left, left_at, lo, n, right, right_at, ro, m, slot, rel):
        tall = n if panels > left_at.size else min(n, 256)
        cols = pl.ds(pl.multiple_of(rel * block + ro, LANES), m)
        over = pl.ds(ro, m)

        def step(i, carry):
            at = pl.ds(pl.multiple_of(lo + i * tall, oct_rows), tall)
            acc[slot, at, cols] = lax.dot_general(
                left[at, left_at], right[over, right_at],
                (((1,), (1,)), ((), ())), preferred_element_type=f32,
            )
            return carry

        if n == tall:
            step(0, 0)
        else:
            lax.fori_loop(0, n // tall, step, 0)

    for role in range(nf):
        @pl.when(f == role)
        def _(role=role):
            for slot, tile in plans[role][1]:
                acc[slot, :, tile * LANES:(tile + 1) * LANES] = jnp.zeros((rows, LANES), f32)

    def valid(slot, o, pp):
        t = o + pp
        low, high = t >= octs - 1, t <= 2 * octs - 1
        if slot == OWN:
            return jnp.logical_or(
                t <= octs - 1,
                jnp.logical_or(
                    jnp.logical_and(odd == 0, high),
                    jnp.logical_and(has_u, t >= 2 * octs - 1),
                ),
            )
        if slot == XG:
            return jnp.logical_and(has_x, jnp.logical_and(low, high))
        upper = jnp.logical_or(t >= 2 * octs - 1, jnp.logical_and(odd == 1, low))
        return jnp.logical_and(has_d, upper)

    def core_copy(slot, o, zd):
        return pltpu.make_async_remote_copy(
            src_ref=away.at[slot, zd, rows_of(o), :], dst_ref=cxin.at[slot, zd, rows_of(o), :],
            send_sem=csend.at[slot, zd, o], recv_sem=crecv.at[slot, zd, o],
            device_id=dev(f, partner), device_id_type=MESH,
        )

    def z_copy(slot, o, zd, source):
        return pltpu.make_async_remote_copy(
            src_ref=zout.at[slot, zd, rows_of(o), :], dst_ref=zin.at[slot, source, rows_of(o), :],
            send_sem=zsend.at[slot, zd, o], recv_sem=zrecv.at[slot, source, o],
            device_id=dev(f, zd * CORES + core), device_id_type=MESH,
        )

    def band(slot, o, zd, side, put):
        lane = pl.multiple_of((o + zd * CORES + side) * LANES, LANES)
        for c in range(8):
            at = pl.ds(pl.multiple_of(o * oct_rows + c * COMP, COMP), COMP)
            if c == 7:
                value = acc[slot, at, pl.ds(pl.multiple_of(lane + LANES, LANES), LANES)]
            else:
                pair = acc[slot, at, pl.ds(lane, 2 * LANES)]
                value = pltpu.roll(pair, 2 * LANES - COMP * (c + 1), 1)[:, :LANES]
            put(at, value)

    def send(slot, o, zd, b):
        def put(at, value):
            away[slot, zd, at, :] = value.astype(bf16)

        band(slot, o, zd, 1 - core, put)
        core_copy(slot, o, zd).start()

    def hold(slot, o, zd, b):
        def put(at, value):
            keep[slot, zd, at, :] = value

        band(slot, o, zd, core, put)

    def straight(o, zd):
        return pltpu.make_async_remote_copy(
            src_ref=zout.at[XG, zd, rows_of(o), :], dst_ref=relay.at[zd, rows_of(o), :],
            send_sem=zsend.at[XG, zd, o], recv_sem=rrecv.at[zd, o],
            device_id=dev(mate, p), device_id_type=MESH,
        )

    def onward(o, zd, source):
        return pltpu.make_async_remote_copy(
            src_ref=relay.at[zd, rows_of(o), :], dst_ref=direct.at[source, rows_of(o), :],
            send_sem=rsend.at[zd, o], recv_sem=drecv.at[source, o],
            device_id=dev(f, zd * CORES + core), device_id_type=MESH,
        )

    def hand_on(slot, o, zd, b):
        straight(o, zd).wait_recv()

        @pl.when(z != zd)
        def _():
            onward(o, zd, z).start()

    def handed(slot, o, zd, b):
        @pl.when(z != zd)
        def _():
            onward(o, zd, z).wait_send()

    def join(slot, o, zd, b):
        at = rows_of(o)
        core_copy(slot, o, zd).wait_recv()
        both = keep[slot, zd, at, :] + cxin[slot, zd, at, :].astype(f32)

        away_now = jnp.logical_and(b == octs, jnp.logical_and(slot == XG, busy))

        @pl.when(jnp.logical_and(z == zd, jnp.logical_not(away_now)))
        def _():
            total[slot, at, :] = both

        @pl.when(jnp.logical_or(z != zd, away_now))
        def _():
            zout[slot, zd, at, :] = both.astype(bf16)

        @pl.when(jnp.logical_and(z != zd, jnp.logical_not(away_now)))
        def _():
            z_copy(slot, o, zd, z).start()

        @pl.when(away_now)
        def _():
            straight(o, zd).start()

    def sent(slot, o, zd, b):
        core_copy(slot, o, zd).wait_send()

    def joined(slot, o, zd, b):
        @pl.when(jnp.logical_or(z != zd, jnp.logical_and(b == octs, jnp.logical_and(slot == XG, busy))))
        def _():
            z_copy(slot, o, zd, z).wait_send()

    def walk(act, chosen, b):
        def step(k, carry):
            code = lax.rem(carry[0], base)
            carry = (lax.div(carry[0], base),) + carry[1:]
            fresh = lax.rem(k + 1, per) == 0
            carry = tuple(jnp.where(fresh, new, old) for new, old in zip(carry[1:] + carry[-1:], carry))
            act(lax.div(code, octs * nz), lax.rem(lax.div(code, nz), octs), lax.rem(code, nz), b)
            return carry

        lax.fori_loop(0, chosen[0], step, tuple(chosen[1:]))

    def each(act, order, b):
        chosen = order[0]
        for bb in range(1, octs + 1):
            chosen = [jnp.where(b == bb, new, old) for new, old in zip(order[bb], chosen)]

        walk(act, chosen, b)

    everything = pl.ds(0, panels)
    first = pl.ds(0, half)
    second = pl.ds(half, half)
    even_now, odd_now = odd == 0, odd == 1

    for load in loads:
        load.wait()
    scale(own, scaled, everything, 0, rows)
    for far in range(1, nz - 1):
        hear(far)
        if far + 1 < nz - 1:
            tell(far + 1)
    gram(scaled, everything, 0, rows, own, everything, 0, rows, OWN, 0)

    def batch(b, carry):
        @pl.when(b > 0)
        def _():
            step = b - 1
            down = pl.multiple_of((octs - 1 - step) * oct_rows, oct_rows)
            up = pl.multiple_of(step * oct_rows, oct_rows)
            to_mate(step).wait_recv()

            @pl.when(odd_now)
            def _():
                scale(xbuf, xs, second, down, oct_rows)
                gram(xs, first, down, oct_rows, own, second, 0, rows, XG, 1)

            @pl.when(even_now)
            def _():
                gram(scaled, first, 0, rows, xbuf, first, down, oct_rows, OWN, 1)

            @pl.when(has_u)
            def _():
                to_lower(step).wait_recv()

                def below_up(i, carry):
                    gram(scaled, first, pl.multiple_of(i * oct_rows, oct_rows), oct_rows, ybuf, first, up, oct_rows, OWN, 2)
                    return carry

                lax.fori_loop(step, octs, below_up, 0)

            @pl.when(jnp.logical_and(has_u, even_now))
            def _():
                scale(xbuf, xs, first, down, oct_rows)

                @pl.when(b == octs)
                def _():
                    gram(xs, first, 0, oct_rows, ybuf, first, 0, rows, XG, 1)
                    gram(xs, first, oct_rows, rows - oct_rows, ybuf, first, rows - oct_rows, oct_rows, XG, 1)

                def cross(j, carry):
                    gram(xs, first, down, oct_rows, ybuf, first, pl.multiple_of(j * oct_rows, oct_rows), oct_rows, XG, 1)
                    gram(xs, first, pl.multiple_of((octs - 1 - j) * oct_rows, oct_rows), oct_rows, ybuf, first, up, oct_rows, XG, 1)
                    return carry

                lax.fori_loop(0, jnp.where(b == octs, 0, b), cross, 0)

            @pl.when(has_d)
            def _():
                to_upper(step).wait_recv()
                scale(ybuf, ys, second, down, oct_rows)

                def up_to_down(i, carry):
                    gram(ys, first, down, oct_rows, own, second, pl.multiple_of(i * oct_rows, oct_rows), oct_rows, DG, 2)
                    return carry

                lax.fori_loop(0, octs - step, up_to_down, 0)

            @pl.when(jnp.logical_and(has_d, odd_now))
            def _():
                @pl.when(b == octs)
                def _():
                    gram(ys, first, 0, oct_rows, xbuf, first, 0, rows, DG, 1)
                    gram(ys, first, oct_rows, rows - oct_rows, xbuf, first, 0, oct_rows, DG, 1)

                def cross(j, carry):
                    there = pl.multiple_of((octs - 1 - j) * oct_rows, oct_rows)
                    gram(ys, first, down, oct_rows, xbuf, first, there, oct_rows, DG, 1)
                    gram(ys, first, there, oct_rows, xbuf, first, down, oct_rows, DG, 1)
                    return carry

                lax.fori_loop(0, jnp.where(b == octs, 0, b), cross, 0)

        each(send, LEAVE, b)
        each(hold, STAY, b)
        each(join, STAY, b)
        return carry

    lax.fori_loop(0, octs + 1, batch, 0)
    walk(hand_on, passing, octs)

    def drain(b, carry):
        each(sent, LEAVE, b)
        each(joined, STAY, b)
        return carry

    lax.fori_loop(0, octs, drain, 0)

    def forward(slot, ff, o):
        return pltpu.make_async_remote_copy(
            src_ref=give.at[slot, rows_of(o), :], dst_ref=fwd.at[slot, rows_of(o), :],
            send_sem=gsend.at[slot, o], recv_sem=grecv.at[slot, o],
            device_id=dev(ff, p), device_id_type=MESH,
        )

    def settle(slot, target):
        def step(o, carry):
            here = valid(slot, o, p)
            if slot == XG:
                here = jnp.logical_and(here, jnp.logical_not(is_late(given, o)))

            @pl.when(here)
            def _():
                value = total[slot, rows_of(o), :]
                for hop in range(1, nz):
                    source = lax.rem(z + hop, nz)
                    z_copy(slot, o, z, source).wait_recv()
                    value = value + zin[slot, source, rows_of(o), :].astype(f32)
                total[slot, rows_of(o), :] = value
                if target is not None:
                    give[slot, rows_of(o), :] = value.astype(bf16)
                    forward(slot, target, o).start()

            if target is None:
                @pl.when(jnp.logical_not(here))
                def _():
                    total[slot, rows_of(o), :] = jnp.zeros((oct_rows, LANES), f32)

            return carry

        lax.fori_loop(0, octs, step, 0)

    def settle_direct(o, carry):
        @pl.when(is_late(got, o))
        def _():
            value = total[OWN, rows_of(o), :] + relay[z, rows_of(o), :].astype(f32)
            for hop in range(1, nz):
                source = lax.rem(z + hop, nz)
                onward(o, z, source).wait_recv()
                value = value + direct[source, rows_of(o), :].astype(f32)
            total[OWN, rows_of(o), :] = value

        return carry

    settle(XG, mate)
    settle(DG, f - 2)
    settle(OWN, None)

    mate_gives = jnp.logical_or(odd == 0, f + 1 < nf)

    def take(slot, giver, comes):
        def step(o, carry):
            @pl.when(comes(o))
            def _():
                forward(slot, giver, o).wait_recv()
                total[OWN, rows_of(o), :] = total[OWN, rows_of(o), :] + fwd[slot, rows_of(o), :].astype(f32)

            return carry

        lax.fori_loop(0, octs, step, 0)

    def from_mate(o):
        t = o + p
        here = jnp.logical_and(mate_gives, jnp.logical_and(t >= octs - 1, t <= 2 * octs - 1))
        return jnp.logical_and(here, jnp.logical_not(is_late(got, o)))

    def from_upper(o):
        t = o + p
        reach = jnp.logical_or(t >= 2 * octs - 1, jnp.logical_and(odd == 1, t >= octs - 1))
        return jnp.logical_and(has_u, reach)

    take(XG, mate, from_mate)
    take(DG, f - 2, from_upper)
    lax.fori_loop(0, octs, settle_direct, 0)

    fin[...] = total[OWN]
    eye = lax.broadcasted_iota(jnp.int32, (freqs, freqs), 0) == lax.broadcasted_iota(
        jnp.int32, (freqs, freqs), 1
    )
    width = jnp.sum(
        jnp.where(eye, jnp.broadcast_to(bw_ref[...].astype(f32), (freqs, freqs)), 0.0), 1, keepdims=True
    )
    width = jnp.broadcast_to(width, (freqs, LANES))
    norm = jnp.float32(1.0 / math.sqrt(panels * npan))
    part = lax.broadcasted_iota(jnp.int32, (freqs, LANES), 1) // COMP
    for h in range(COMP // 8):
        values = [fin[pl.ds(h * 8 + a, freqs, stride=COMP), :] for a in range(8)]
        for bit in (1, 2, 4):
            upper = lax.rem(part // bit, 2) == 1
            fresh = list(values)
            for i in range(8):
                if i & bit:
                    continue
                j = i | bit
                fresh[i] = jnp.where(upper, pltpu.roll(values[j], COMP * bit, 1), values[i])
                fresh[j] = jnp.where(upper, values[j], pltpu.roll(values[i], LANES - COMP * bit, 1))
            values = fresh
        for k in range(8):
            offset = (p * 8 + k + 1).astype(f32)
            live = offset <= width
            start = (k * (COMP // 8) + h) * LANES
            out_ref[:, start:start + LANES] = jnp.where(live, values[k] * norm, 0.0)

    drain(octs, 0)
    walk(handed, passing, octs)

    def close(o, carry):
        to_mate(o).wait_send()

        @pl.when(has_d)
        def _():
            to_lower(o).wait_send()

        @pl.when(has_u)
        def _():
            to_upper(o).wait_send()

        @pl.when(jnp.logical_and(valid(XG, o, p), jnp.logical_not(is_late(given, o))))
        def _():
            forward(XG, mate, o).wait_send()

        @pl.when(valid(DG, o, p))
        def _():
            forward(DG, f - 2, o).wait_send()

        return carry

    lax.fori_loop(0, octs, close, 0)


def fused(nf, npan, fields, quad_index, band_width):
    freqs, comp, panels = fields.shape
    rows = freqs * comp
    nz = npan // CORES
    half = panels // 2
    octs = freqs // 8
    out_cols = REACH * freqs * comp * comp // npan
    bf16, f32 = jnp.bfloat16, jnp.float32
    dma = pltpu.SemaphoreType.DMA
    vmem = pl.BlockSpec(memory_space=pltpu.VMEM)
    return pl.pallas_call(
        functools.partial(kernel, nf, npan),
        out_shape=jax.ShapeDtypeStruct((freqs, out_cols), f32),
        in_specs=[pl.BlockSpec(memory_space=pl.ANY)] * 3,
        out_specs=vmem,
        scratch_shapes=[
            pltpu.VMEM((rows, panels), bf16),
            pltpu.VMEM((rows, panels), bf16),
            pltpu.VMEM((rows, half), bf16),
            pltpu.VMEM((rows, half), bf16),
            pltpu.VMEM((rows, half), bf16),
            pltpu.VMEM((rows, half), bf16),
            pltpu.VMEM((3, rows, (REACH + 1) * rows), f32),
            pltpu.VMEM((3, nz, rows, LANES), f32),
            pltpu.VMEM((3, nz, rows, LANES), bf16),
            pltpu.VMEM((3, nz, rows, LANES), bf16),
            pltpu.VMEM((3, nz, rows, LANES), bf16),
            pltpu.VMEM((3, nz, rows, LANES), bf16),
            pltpu.VMEM((3, rows, LANES), f32),
            pltpu.VMEM((3, rows, LANES), bf16),
            pltpu.VMEM((3, rows, LANES), bf16),
            pltpu.VMEM((rows, LANES), f32),
            pltpu.VMEM((nz, rows, LANES), bf16),
            pltpu.VMEM((nz, rows, LANES), bf16),
            pltpu.VMEM((1, panels), jnp.int32),
            pltpu.VMEM((1, freqs), jnp.int32),
            pltpu.SemaphoreType.REGULAR((2, max(nz - 2, 1))),
            dma((3,)),
            dma((2, octs)), dma((2, octs)),
            dma((3, nz, octs)), dma((3, nz, octs)),
            dma((3, nz, octs)), dma((3, nz, octs)),
            dma((3, octs)), dma((3, octs)),
            dma((nz, octs)), dma((nz, octs)), dma((nz, octs)),
        ],
        compiler_params=pltpu.CompilerParams(
            collective_id=0, has_side_effects=True, vmem_limit_bytes=58 * 1024 * 1024
        ),
    )(fields.reshape(rows, panels), quad_index.reshape(1, panels), band_width.reshape(1, freqs))


def local(nf, npan, fields, quad_index, band_width):
    freqs, comp, panels = fields.shape
    share = REACH * freqs * comp // npan
    fits = nf == 2 * REACH and npan % CORES == 0 and share == LANES and freqs % 8 == 0 and panels % (4 * LANES) == 0
    if not fits:
        return plain(fields, quad_index, band_width)
    return fused(nf, npan, fields, quad_index, band_width)


def solution(mesh):
    placed = (P("freq", None, "panel"), P("panel"), P("freq"))
    return jax.shard_map(
        functools.partial(local, mesh.shape["freq"], mesh.shape["panel"]),
        mesh=mesh, in_specs=placed, out_specs=P("freq", "panel"), check_vma=False,
    )
```

```python
import functools
import math

import jax
import jax.numpy as jnp
from jax import lax
from jax.experimental import pallas as pl
from jax.experimental.pallas import tpu as pltpu
from jax.sharding import PartitionSpec as P

COMP = 16
REACH = 2
LANES = 128
CORES = 2
MESH = pl.DeviceIdType.MESH

QUAD_TABLE = (0.2, 0.45, 0.8, 1.1, 1.6, 2.3)


def shifted(x, axis, by):
    devices = lax.axis_size(axis)
    pairs = [(i, i + by) for i in range(devices) if 0 <= i + by < devices]
    return lax.ppermute(x, axis, pairs)


def plain(fields, quad_index, band_width):
    freq_local = fields.shape[0]
    panel_local = fields.shape[2]
    band = REACH * freq_local
    table = jnp.asarray(QUAD_TABLE, jnp.float32)
    matches = quad_index[None, :] == jnp.arange(6, dtype=jnp.int32)[:, None]
    weight = jnp.sum(jnp.where(matches, table[:, None], jnp.float32(0.0)), 0)
    scaled = (fields.astype(jnp.float32) * weight).astype(jnp.bfloat16)
    own_rows = scaled.reshape(freq_local * COMP, panel_local)
    partners = [fields]
    for distance in range(1, REACH + 1):
        partners.append(shifted(fields, "freq", -distance))
    grams = []
    for partner in partners:
        grams.append(
            lax.dot_general(
                own_rows,
                partner.reshape(freq_local * COMP, panel_local),
                (((1,), (1,)), ((), ())),
                preferred_element_type=jnp.float32,
            )
        )
    stacked = jnp.concatenate(grams, 1).reshape(freq_local, COMP, (REACH + 1) * freq_local, COMP)

    def pick_band(block, row_index):
        return lax.dynamic_slice_in_dim(block, row_index + 1, band, 1)

    picked = jax.vmap(pick_band)(stacked, jnp.arange(freq_local, dtype=jnp.int32))
    picked = picked.transpose(0, 2, 1, 3)
    offsets = jnp.arange(band, dtype=jnp.int32) + 1
    live_mask = offsets[None, :] <= band_width[:, None]
    picked = jnp.where(live_mask[:, :, None, None], picked, jnp.float32(0.0))
    panels_total = panel_local * lax.axis_size("panel")
    terms = picked.reshape(freq_local, band * COMP * COMP) * jnp.float32(
        1.0 / math.sqrt(panels_total)
    )
    return lax.psum_scatter(terms, "panel", scatter_dimension=1, tiled=True)


OWN, XG, DG = 0, 1, 2


def plan(role, octs, npan):
    even, low = role % 2 == 0, role < 2

    def due(slot, row, col):
        block, col = divmod(col, octs)
        x_row, x_col = octs - row, octs - col
        y_row, y_col = x_row, col + 1 if low else x_col
        if slot == OWN:
            if block == 0:
                return 0
            if block == 1 and even:
                return x_col
            if block == 2 and low:
                return y_col
        if slot == XG and block == 1:
            if not even:
                return x_row
            if low:
                return max(x_row, y_col)
        if slot == DG and not low:
            if block == 2:
                return y_row
            if block == 1 and not even:
                return max(y_row, x_col)
        return None

    batches = [[[] for _ in range(octs + 1)] for _ in range(CORES)]
    blank = set()
    for slot in (XG, DG, OWN):
        for o in range(octs):
            for pp in range(npan):
                t = o + pp
                times = [due(slot, o, t), due(slot, o, t + 1)]
                if times == [None, None]:
                    continue
                blank.update((slot, t + k) for k in range(2) if times[k] is None)
                last = max(time for time in times if time is not None)
                batches[pp % CORES][last].append((slot, o, pp // CORES))
    return batches, sorted(blank)


def kernel(
    nf, npan, f_hbm, q_hbm, out_ref,
    own, scaled, xbuf, ybuf, xs, ys, acc, keep, away, cxin, zout, zin, total, give, fwd, relay, direct,
    q_ref, near, local_sem, fsend, frecv, csend, crecv, zsend, zrecv, gsend, grecv, rsend, rrecv, drecv,
):
    rows, panels = own.shape
    half = panels // 2
    block = rows
    oct_rows = 8 * COMP
    octs = rows // oct_rows
    nz = npan // CORES
    f32, bf16 = jnp.float32, jnp.bfloat16

    f = lax.axis_index("freq")
    p = lax.axis_index("panel")
    z, core = p // CORES, lax.rem(p, CORES)
    odd = lax.rem(f, 2)
    mate = f + 1 - 2 * odd
    has_u = f + 2 < nf
    has_d = f >= 2
    has_x = jnp.logical_or(odd == 1, has_u)
    partner = p + 1 - 2 * core

    def dev(ff, pp):
        return {"freq": ff, "panel": pp}


    barrier = pltpu.get_barrier_semaphore()
    below, above = z > 0, z < nz - 1

    def greet(ff, pp):
        pl.semaphore_signal(barrier, inc=1, device_id=dev(ff, pp), device_id_type=MESH)

    greet(mate, p)
    greet(f, partner)

    @pl.when(below)
    def _():
        greet(f, p - CORES)

    @pl.when(above)
    def _():
        greet(f, p + CORES)

    @pl.when(has_u)
    def _():
        greet(f + 2, p)

    @pl.when(has_d)
    def _():
        greet(f - 2, p)

    loads = [
        pltpu.make_async_copy(f_hbm, own, local_sem.at[0]),
        pltpu.make_async_copy(q_hbm, q_ref, local_sem.at[1]),
    ]
    for load in loads:
        load.start()

    count = 2
    for there in (below, above, has_u, has_d):
        count = count + jnp.where(there, 1, 0)
    pl.semaphore_wait(barrier, count)

    def half_at(which):
        return pl.ds(pl.multiple_of(which * half, LANES), half)

    def rows_of(o, n=1):
        return pl.ds(pl.multiple_of(o * oct_rows, oct_rows), n * oct_rows)

    def field_copy(which, dst, slot, ff, step, o):
        return pltpu.make_async_remote_copy(
            src_ref=f_hbm.at[rows_of(o), half_at(which)], dst_ref=dst.at[rows_of(o), :],
            send_sem=fsend.at[slot, step], recv_sem=frecv.at[slot, step],
            device_id=dev(ff, p), device_id_type=MESH,
        )

    def to_mate(step):
        return field_copy(1 - odd, xbuf, 0, mate, step, octs - 1 - step)

    def to_lower(step):
        return field_copy(0, ybuf, 1, f - 2, step, step)

    def to_upper(step):
        return field_copy(1, ybuf, 1, f + 2, step, octs - 1 - step)

    def depart(step, carry):
        to_mate(step).start()

        @pl.when(has_d)
        def _():
            to_lower(step).start()

        @pl.when(has_u)
        def _():
            to_upper(step).start()

        return carry

    lax.fori_loop(0, octs, depart, 0)

    plans = [plan(role, octs, npan) for role in range(nf)]
    base = 1
    while base < 3 * octs * nz:
        base *= 2
    per = 1
    while base ** (per + 1) <= 2 ** 31:
        per += 1
    most = max(len(found) for lists, _ in plans for side in lists for found in side)
    words = max(-(-most // per), 1)

    def packed(found, w):
        value = 0
        for slot, o, zd in reversed(found[w * per:(w + 1) * per]):
            value = value * base + (slot * octs + o) * nz + zd
        return value

    def mine(seat, of):
        value = jnp.int32(0)
        for role in range(nf):
            for side in range(CORES):
                value = jnp.where(seat == role * CORES + side, jnp.int32(of(role, side)), value)
        return value

    def group(role, side, b, own_tiles):
        return [tile for tile in plans[role][0][side][b] if (tile[0] == OWN) == own_tiles]

    orders = []
    for seat in (f * CORES + 1 - core, f * CORES + core):
        for kind in (False, True):
            orders.append([
                [mine(seat, lambda role, side: len(group(role, side, b, kind)))]
                + [mine(seat, lambda role, side: packed(group(role, side, b, kind), w)) for w in range(words)]
                for b in range(octs + 1)
            ])
    LEAVE_CROSS, LEAVE_OWN, STAY_CROSS, STAY_OWN = orders
    busy = jnp.logical_or(jnp.logical_and(has_u, odd == 0), jnp.logical_and(has_d, odd == 1))

    def crossing(role, side):
        busy = (role < 2) == (role % 2 == 0)
        return [tile for tile in plans[role][0][side][octs] if busy and tile[0] == XG]

    passing = [mine(mate * CORES + core, lambda role, side: len(crossing(role, side)))]
    passing += [mine(mate * CORES + core, lambda role, side: packed(crossing(role, side), w)) for w in range(words)]

    def tell(far):
        @pl.when(jnp.logical_and(above, z >= far))
        def _():
            pl.semaphore_signal(near.at[0, far - 1], inc=1, device_id=dev(f, p + CORES), device_id_type=MESH)

        @pl.when(jnp.logical_and(below, z + far < nz))
        def _():
            pl.semaphore_signal(near.at[1, far - 1], inc=1, device_id=dev(f, p - CORES), device_id_type=MESH)

    def hear(far):
        @pl.when(z > far)
        def _():
            pl.semaphore_wait(near.at[0, far - 1], 1)

        @pl.when(z + 1 + far < nz)
        def _():
            pl.semaphore_wait(near.at[1, far - 1], 1)

    def late_bits(giver):
        value = jnp.int32(0)
        for role in range(nf):
            for pp in range(npan):
                bits = sum(2 ** o for _, o, zd in crossing(role, pp % CORES) if zd == pp // CORES)
                if bits:
                    value = jnp.where(jnp.logical_and(giver == role, p == pp), jnp.int32(bits), value)
        return value

    def is_late(bits, o):
        picked = jnp.int32(0)
        for oo in range(octs):
            picked = jnp.where(o == oo, lax.rem(lax.div(bits, 2 ** oo), 2), picked)
        return picked == 1

    given = late_bits(f)
    got = late_bits(mate)
    tell(1)

    def weight_at(where):
        index = q_ref[:, where]
        w = jnp.zeros(index.shape, f32)
        for value, entry in enumerate(QUAD_TABLE):
            w = jnp.where(index == value, jnp.float32(entry), w)
        return w

    def scale(src, dst, where, start, count):
        w = weight_at(where)

        def step(i, carry):
            at = pl.ds(pl.multiple_of(start + i * 32, 32), 32)
            dst[at, :] = (src[at, :].astype(f32) * w).astype(bf16)
            return carry

        lax.fori_loop(0, count // 32, step, 0)

    def gram(left, left_at, lo, n, right, right_at, ro, m, slot, rel):
        tall = n if panels > left_at.size else min(n, 256)
        cols = pl.ds(pl.multiple_of(rel * block + ro, LANES), m)
        over = pl.ds(ro, m)

        def step(i, carry):
            at = pl.ds(pl.multiple_of(lo + i * tall, oct_rows), tall)
            acc[slot, at, cols] = lax.dot_general(
                left[at, left_at], right[over, right_at],
                (((1,), (1,)), ((), ())), preferred_element_type=f32,
            )
            return carry

        if n == tall:
            step(0, 0)
        else:
            lax.fori_loop(0, n // tall, step, 0)

    for role in range(nf):
        @pl.when(f == role)
        def _(role=role):
            for slot, tile in plans[role][1]:
                acc[slot, :, tile * LANES:(tile + 1) * LANES] = jnp.zeros((rows, LANES), f32)

    def valid(slot, o, pp):
        t = o + pp
        low, high = t >= octs - 1, t <= 2 * octs - 1
        if slot == OWN:
            return jnp.logical_or(
                t <= octs - 1,
                jnp.logical_or(
                    jnp.logical_and(odd == 0, high),
                    jnp.logical_and(has_u, t >= 2 * octs - 1),
                ),
            )
        if slot == XG:
            return jnp.logical_and(has_x, jnp.logical_and(low, high))
        upper = jnp.logical_or(t >= 2 * octs - 1, jnp.logical_and(odd == 1, low))
        return jnp.logical_and(has_d, upper)

    def core_copy(slot, o, zd):
        return pltpu.make_async_remote_copy(
            src_ref=away.at[slot, zd, rows_of(o), :], dst_ref=cxin.at[slot, zd, rows_of(o), :],
            send_sem=csend.at[slot, zd, o], recv_sem=crecv.at[slot, zd, o],
            device_id=dev(f, partner), device_id_type=MESH,
        )

    def z_copy(slot, o, zd, source):
        return pltpu.make_async_remote_copy(
            src_ref=zout.at[slot, zd, rows_of(o), :], dst_ref=zin.at[slot, source, rows_of(o), :],
            send_sem=zsend.at[slot, zd, o], recv_sem=zrecv.at[slot, source, o],
            device_id=dev(f, zd * CORES + core), device_id_type=MESH,
        )

    def band(slot, o, zd, side, put):
        lane = pl.multiple_of((o + zd * CORES + side) * LANES, LANES)
        for c in range(8):
            at = pl.ds(pl.multiple_of(o * oct_rows + c * COMP, COMP), COMP)
            if c == 7:
                value = acc[slot, at, pl.ds(pl.multiple_of(lane + LANES, LANES), LANES)]
            else:
                pair = acc[slot, at, pl.ds(lane, 2 * LANES)]
                value = pltpu.roll(pair, 2 * LANES - COMP * (c + 1), 1)[:, :LANES]
            put(at, value)

    def send(slot, o, zd, b):
        def put(at, value):
            away[slot, zd, at, :] = value.astype(bf16)

        band(slot, o, zd, 1 - core, put)
        core_copy(slot, o, zd).start()

    def hold(slot, o, zd, b):
        def put(at, value):
            keep[slot, zd, at, :] = value

        band(slot, o, zd, core, put)

    def straight(o, zd):
        return pltpu.make_async_remote_copy(
            src_ref=zout.at[XG, zd, rows_of(o), :], dst_ref=relay.at[zd, rows_of(o), :],
            send_sem=zsend.at[XG, zd, o], recv_sem=rrecv.at[zd, o],
            device_id=dev(mate, p), device_id_type=MESH,
        )

    def onward(o, zd, source):
        return pltpu.make_async_remote_copy(
            src_ref=relay.at[zd, rows_of(o), :], dst_ref=direct.at[source, rows_of(o), :],
            send_sem=rsend.at[zd, o], recv_sem=drecv.at[source, o],
            device_id=dev(f, zd * CORES + core), device_id_type=MESH,
        )

    def hand_on(slot, o, zd, b):
        straight(o, zd).wait_recv()

        @pl.when(z != zd)
        def _():
            onward(o, zd, z).start()

    def handed(slot, o, zd, b):
        @pl.when(z != zd)
        def _():
            onward(o, zd, z).wait_send()

    def join(slot, o, zd, b):
        at = rows_of(o)
        core_copy(slot, o, zd).wait_recv()
        both = keep[slot, zd, at, :] + cxin[slot, zd, at, :].astype(f32)

        away_now = jnp.logical_and(b == octs, jnp.logical_and(slot == XG, busy))

        @pl.when(jnp.logical_and(z == zd, jnp.logical_not(away_now)))
        def _():
            total[slot, at, :] = both

        @pl.when(jnp.logical_or(z != zd, away_now))
        def _():
            zout[slot, zd, at, :] = both.astype(bf16)

        @pl.when(jnp.logical_and(z != zd, jnp.logical_not(away_now)))
        def _():
            z_copy(slot, o, zd, z).start()

        @pl.when(away_now)
        def _():
            straight(o, zd).start()

    def sent(slot, o, zd, b):
        core_copy(slot, o, zd).wait_send()

    def joined(slot, o, zd, b):
        @pl.when(jnp.logical_or(z != zd, jnp.logical_and(b == octs, jnp.logical_and(slot == XG, busy))))
        def _():
            z_copy(slot, o, zd, z).wait_send()

    def walk(act, chosen, b):
        def step(k, carry):
            code = lax.rem(carry[0], base)
            carry = (lax.div(carry[0], base),) + carry[1:]
            fresh = lax.rem(k + 1, per) == 0
            carry = tuple(jnp.where(fresh, new, old) for new, old in zip(carry[1:] + carry[-1:], carry))
            act(lax.div(code, octs * nz), lax.rem(lax.div(code, nz), octs), lax.rem(code, nz), b)
            return carry

        lax.fori_loop(0, chosen[0], step, tuple(chosen[1:]))

    def each(act, order, b):
        chosen = order[0]
        for bb in range(1, octs + 1):
            chosen = [jnp.where(b == bb, new, old) for new, old in zip(order[bb], chosen)]

        walk(act, chosen, b)

    everything = pl.ds(0, panels)
    first = pl.ds(0, half)
    second = pl.ds(half, half)
    even_now, odd_now = odd == 0, odd == 1

    for load in loads:
        load.wait()
    scale(own, scaled, everything, 0, rows)
    for far in range(1, nz - 1):
        hear(far)
        if far + 1 < nz - 1:
            tell(far + 1)
    gram(scaled, everything, 0, rows, own, everything, 0, rows, OWN, 0)

    def batch(b, carry):
        step = jnp.maximum(b - 1, 0)
        down = pl.multiple_of((octs - 1 - step) * oct_rows, oct_rows)
        up = pl.multiple_of(step * oct_rows, oct_rows)

        @pl.when(b > 0)
        def _():
            to_mate(step).wait_recv()

            @pl.when(odd_now)
            def _():
                scale(xbuf, xs, second, down, oct_rows)
                gram(xs, first, down, oct_rows, own, second, 0, rows, XG, 1)

            @pl.when(has_u)
            def _():
                to_lower(step).wait_recv()

            @pl.when(jnp.logical_and(has_u, even_now))
            def _():
                scale(xbuf, xs, first, down, oct_rows)

                @pl.when(b == octs)
                def _():
                    gram(xs, first, 0, oct_rows, ybuf, first, 0, rows, XG, 1)
                    gram(xs, first, oct_rows, rows - oct_rows, ybuf, first, rows - oct_rows, oct_rows, XG, 1)

                def cross(j, carry):
                    there = pl.multiple_of((octs - 1 - j) * oct_rows, oct_rows)
                    gram(xs, first, down, oct_rows, ybuf, first, pl.multiple_of(j * oct_rows, oct_rows), oct_rows, XG, 1)
                    gram(xs, first, there, oct_rows, ybuf, first, up, oct_rows, XG, 1)
                    return carry

                lax.fori_loop(0, jnp.where(b == octs, 0, b), cross, 0)

            @pl.when(has_d)
            def _():
                to_upper(step).wait_recv()
                scale(ybuf, ys, second, down, oct_rows)

                def up_to_down(i, carry):
                    gram(ys, first, down, oct_rows, own, second, pl.multiple_of(i * oct_rows, oct_rows), oct_rows, DG, 2)
                    return carry

                lax.fori_loop(0, octs - step, up_to_down, 0)

            @pl.when(jnp.logical_and(has_d, odd_now))
            def _():
                @pl.when(b == octs)
                def _():
                    gram(ys, first, 0, oct_rows, xbuf, first, 0, rows, DG, 1)
                    gram(ys, first, oct_rows, rows - oct_rows, xbuf, first, 0, oct_rows, DG, 1)

                def cross(j, carry):
                    there = pl.multiple_of((octs - 1 - j) * oct_rows, oct_rows)
                    gram(ys, first, down, oct_rows, xbuf, first, there, oct_rows, DG, 1)
                    gram(ys, first, there, oct_rows, xbuf, first, down, oct_rows, DG, 1)
                    return carry

                lax.fori_loop(0, jnp.where(b == octs, 0, b), cross, 0)

        each(send, LEAVE_CROSS, b)

        @pl.when(b > 0)
        def _():
            @pl.when(even_now)
            def _():
                gram(scaled, first, 0, rows, xbuf, first, down, oct_rows, OWN, 1)

            @pl.when(has_u)
            def _():
                def below_up(i, carry):
                    gram(scaled, first, pl.multiple_of(i * oct_rows, oct_rows), oct_rows, ybuf, first, up, oct_rows, OWN, 2)
                    return carry

                lax.fori_loop(step, octs, below_up, 0)

        each(send, LEAVE_OWN, b)
        each(hold, STAY_CROSS, b)
        each(join, STAY_CROSS, b)
        each(hold, STAY_OWN, b)
        each(join, STAY_OWN, b)
        return carry

    lax.fori_loop(0, octs + 1, batch, 0)
    walk(hand_on, passing, octs)

    def drain(b, carry):
        for order in (LEAVE_CROSS, LEAVE_OWN):
            each(sent, order, b)
        for order in (STAY_CROSS, STAY_OWN):
            each(joined, order, b)
        return carry

    lax.fori_loop(0, octs, drain, 0)

    def forward(slot, ff, o):
        return pltpu.make_async_remote_copy(
            src_ref=give.at[slot, rows_of(o), :], dst_ref=fwd.at[slot, rows_of(o), :],
            send_sem=gsend.at[slot, o], recv_sem=grecv.at[slot, o],
            device_id=dev(ff, p), device_id_type=MESH,
        )

    def settle(slot, target):
        def step(o, carry):
            here = valid(slot, o, p)
            if slot == XG:
                here = jnp.logical_and(here, jnp.logical_not(is_late(given, o)))

            @pl.when(here)
            def _():
                value = total[slot, rows_of(o), :]
                for hop in range(1, nz):
                    source = lax.rem(z + hop, nz)
                    z_copy(slot, o, z, source).wait_recv()
                    value = value + zin[slot, source, rows_of(o), :].astype(f32)
                total[slot, rows_of(o), :] = value
                if target is not None:
                    give[slot, rows_of(o), :] = value.astype(bf16)
                    forward(slot, target, o).start()

            if target is None:
                @pl.when(jnp.logical_not(here))
                def _():
                    total[slot, rows_of(o), :] = jnp.zeros((oct_rows, LANES), f32)

            return carry

        lax.fori_loop(0, octs, step, 0)

    def settle_direct(o, carry):
        @pl.when(is_late(got, o))
        def _():
            value = total[OWN, rows_of(o), :] + relay[z, rows_of(o), :].astype(f32)
            for hop in range(1, nz):
                source = lax.rem(z + hop, nz)
                onward(o, z, source).wait_recv()
                value = value + direct[source, rows_of(o), :].astype(f32)
            total[OWN, rows_of(o), :] = value

        return carry

    settle(XG, mate)
    settle(DG, f - 2)
    settle(OWN, None)

    mate_gives = jnp.logical_or(odd == 0, f + 1 < nf)

    def take(slot, giver, comes):
        def step(o, carry):
            @pl.when(comes(o))
            def _():
                forward(slot, giver, o).wait_recv()
                total[OWN, rows_of(o), :] = total[OWN, rows_of(o), :] + fwd[slot, rows_of(o), :].astype(f32)

            return carry

        lax.fori_loop(0, octs, step, 0)

    def from_mate(o):
        t = o + p
        here = jnp.logical_and(mate_gives, jnp.logical_and(t >= octs - 1, t <= 2 * octs - 1))
        return jnp.logical_and(here, jnp.logical_not(is_late(got, o)))

    def from_upper(o):
        t = o + p
        reach = jnp.logical_or(t >= 2 * octs - 1, jnp.logical_and(odd == 1, t >= octs - 1))
        return jnp.logical_and(has_u, reach)

    take(XG, mate, from_mate)
    take(DG, f - 2, from_upper)
    lax.fori_loop(0, octs, settle_direct, 0)

    out_ref[...] = total[OWN]

    drain(octs, 0)
    walk(handed, passing, octs)

    def close(o, carry):
        to_mate(o).wait_send()

        @pl.when(has_d)
        def _():
            to_lower(o).wait_send()

        @pl.when(has_u)
        def _():
            to_upper(o).wait_send()

        @pl.when(jnp.logical_and(valid(XG, o, p), jnp.logical_not(is_late(given, o))))
        def _():
            forward(XG, mate, o).wait_send()

        @pl.when(valid(DG, o, p))
        def _():
            forward(DG, f - 2, o).wait_send()

        return carry

    lax.fori_loop(0, octs, close, 0)


def finalize(panels_total, bw_ref, sum_ref, blocks_ref):
    f32 = jnp.float32
    freqs = blocks_ref.shape[0]
    p = lax.axis_index("panel")
    eye = lax.broadcasted_iota(jnp.int32, (freqs, freqs), 0) == lax.broadcasted_iota(
        jnp.int32, (freqs, freqs), 1
    )
    width = jnp.sum(
        jnp.where(eye, jnp.broadcast_to(bw_ref[...].astype(f32), (freqs, freqs)), 0.0), 1, keepdims=True
    )
    width = jnp.broadcast_to(width, (freqs, LANES))
    norm = jnp.float32(1.0 / math.sqrt(panels_total))
    part = lax.broadcasted_iota(jnp.int32, (freqs, LANES), 1) // COMP
    for h in range(COMP // 8):
        values = [sum_ref[pl.ds(h * 8 + a, freqs, stride=COMP), :] for a in range(8)]
        for bit in (1, 2, 4):
            upper = lax.rem(part // bit, 2) == 1
            fresh = list(values)
            for i in range(8):
                if i & bit:
                    continue
                j = i | bit
                fresh[i] = jnp.where(upper, pltpu.roll(values[j], COMP * bit, 1), values[i])
                fresh[j] = jnp.where(upper, values[j], pltpu.roll(values[i], LANES - COMP * bit, 1))
            values = fresh
        for k in range(8):
            offset = (p * 8 + k + 1).astype(f32)
            live = offset <= width
            start = (k * (COMP // 8) + h) * LANES
            blocks_ref[:, start:start + LANES] = jnp.where(live, values[k] * norm, 0.0)


def fused(nf, npan, fields, quad_index, band_width):
    freqs, comp, panels = fields.shape
    rows = freqs * comp
    nz = npan // CORES
    half = panels // 2
    octs = freqs // 8
    out_cols = REACH * freqs * comp * comp // npan
    bf16, f32 = jnp.bfloat16, jnp.float32
    dma = pltpu.SemaphoreType.DMA
    vmem = pl.BlockSpec(memory_space=pltpu.VMEM)
    sums = pl.pallas_call(
        functools.partial(kernel, nf, npan),
        out_shape=jax.ShapeDtypeStruct((rows, LANES), f32),
        in_specs=[pl.BlockSpec(memory_space=pltpu.HBM)] * 2,
        out_specs=vmem,
        scratch_shapes=[
            pltpu.VMEM((rows, panels), bf16),
            pltpu.VMEM((rows, panels), bf16),
            pltpu.VMEM((rows, half), bf16),
            pltpu.VMEM((rows, half), bf16),
            pltpu.VMEM((rows, half), bf16),
            pltpu.VMEM((rows, half), bf16),
            pltpu.VMEM((3, rows, (REACH + 1) * rows), f32),
            pltpu.VMEM((3, nz, rows, LANES), f32),
            pltpu.VMEM((3, nz, rows, LANES), bf16),
            pltpu.VMEM((3, nz, rows, LANES), bf16),
            pltpu.VMEM((3, nz, rows, LANES), bf16),
            pltpu.VMEM((3, nz, rows, LANES), bf16),
            pltpu.VMEM((3, rows, LANES), f32),
            pltpu.VMEM((3, rows, LANES), bf16),
            pltpu.VMEM((3, rows, LANES), bf16),
            pltpu.VMEM((nz, rows, LANES), bf16),
            pltpu.VMEM((nz, rows, LANES), bf16),
            pltpu.VMEM((1, panels), jnp.int32),
            pltpu.SemaphoreType.REGULAR((2, max(nz - 2, 1))),
            dma((2,)),
            dma((2, octs)), dma((2, octs)),
            dma((3, nz, octs)), dma((3, nz, octs)),
            dma((3, nz, octs)), dma((3, nz, octs)),
            dma((3, octs)), dma((3, octs)),
            dma((nz, octs)), dma((nz, octs)), dma((nz, octs)),
        ],
        compiler_params=pltpu.CompilerParams(
            collective_id=0, has_side_effects=True, vmem_limit_bytes=40 * 1024 * 1024
        ),
    )(
        pltpu.with_memory_space_constraint(fields.reshape(rows, panels), pltpu.HBM),
        pltpu.with_memory_space_constraint(quad_index.reshape(1, panels), pltpu.HBM),
    )
    return pl.pallas_call(
        functools.partial(finalize, panels * npan),
        out_shape=jax.ShapeDtypeStruct((freqs, out_cols), f32),
        in_specs=[vmem, vmem],
        out_specs=vmem,
        compiler_params=pltpu.CompilerParams(vmem_limit_bytes=8 * 1024 * 1024),
    )(band_width.reshape(1, freqs), sums)


def local(nf, npan, fields, quad_index, band_width):
    freqs, comp, panels = fields.shape
    share = REACH * freqs * comp // npan
    fits = nf == 2 * REACH and npan % CORES == 0 and share == LANES and freqs % 8 == 0 and panels % (4 * LANES) == 0
    if not fits:
        return plain(fields, quad_index, band_width)
    return fused(nf, npan, fields, quad_index, band_width)


def solution(mesh):
    placed = (P("freq", None, "panel"), P("panel"), P("freq"))
    return jax.shard_map(
        functools.partial(local, mesh.shape["freq"], mesh.shape["panel"]),
        mesh=mesh, in_specs=placed, out_specs=P("freq", "panel"), check_vma=False,
    )
```

```python
import functools
import math

import jax
import jax.numpy as jnp
from jax import lax
from jax.experimental import pallas as pl
from jax.experimental.pallas import tpu as pltpu
from jax.sharding import PartitionSpec as P

COMP = 16
REACH = 2
LANES = 128
CORES = 2
MESH = pl.DeviceIdType.MESH

QUAD_TABLE = (0.2, 0.45, 0.8, 1.1, 1.6, 2.3)


def shifted(x, axis, by):
    devices = lax.axis_size(axis)
    pairs = [(i, i + by) for i in range(devices) if 0 <= i + by < devices]
    return lax.ppermute(x, axis, pairs)


def plain(fields, quad_index, band_width):
    freq_local = fields.shape[0]
    panel_local = fields.shape[2]
    band = REACH * freq_local
    table = jnp.asarray(QUAD_TABLE, jnp.float32)
    matches = quad_index[None, :] == jnp.arange(6, dtype=jnp.int32)[:, None]
    weight = jnp.sum(jnp.where(matches, table[:, None], jnp.float32(0.0)), 0)
    scaled = (fields.astype(jnp.float32) * weight).astype(jnp.bfloat16)
    own_rows = scaled.reshape(freq_local * COMP, panel_local)
    partners = [fields]
    for distance in range(1, REACH + 1):
        partners.append(shifted(fields, "freq", -distance))
    grams = []
    for partner in partners:
        grams.append(
            lax.dot_general(
                own_rows,
                partner.reshape(freq_local * COMP, panel_local),
                (((1,), (1,)), ((), ())),
                preferred_element_type=jnp.float32,
            )
        )
    stacked = jnp.concatenate(grams, 1).reshape(freq_local, COMP, (REACH + 1) * freq_local, COMP)

    def pick_band(block, row_index):
        return lax.dynamic_slice_in_dim(block, row_index + 1, band, 1)

    picked = jax.vmap(pick_band)(stacked, jnp.arange(freq_local, dtype=jnp.int32))
    picked = picked.transpose(0, 2, 1, 3)
    offsets = jnp.arange(band, dtype=jnp.int32) + 1
    live_mask = offsets[None, :] <= band_width[:, None]
    picked = jnp.where(live_mask[:, :, None, None], picked, jnp.float32(0.0))
    panels_total = panel_local * lax.axis_size("panel")
    terms = picked.reshape(freq_local, band * COMP * COMP) * jnp.float32(
        1.0 / math.sqrt(panels_total)
    )
    return lax.psum_scatter(terms, "panel", scatter_dimension=1, tiled=True)


OWN, XG, DG = 0, 1, 2


def plan(role, octs, npan):
    even, low = role % 2 == 0, role < 2

    def due(slot, row, col):
        block, col = divmod(col, octs)
        x_row, x_col = octs - row, octs - col
        y_row, y_col = x_row, col + 1 if low else x_col
        if slot == OWN:
            if block == 0:
                return 0
            if block == 1 and even:
                return x_col
            if block == 2 and low:
                return y_col
        if slot == XG and block == 1:
            if not even:
                return x_row
            if low:
                return max(x_row, y_col)
        if slot == DG and not low:
            if block == 2:
                return y_row
            if block == 1 and not even:
                return max(y_row, x_col)
        return None

    batches = [[[] for _ in range(octs + 1)] for _ in range(CORES)]
    blank = set()
    for slot in (XG, DG, OWN):
        for o in range(octs):
            for pp in range(npan):
                t = o + pp
                times = [due(slot, o, t), due(slot, o, t + 1)]
                if times == [None, None]:
                    continue
                blank.update((slot, t + k) for k in range(2) if times[k] is None)
                last = max(time for time in times if time is not None)
                batches[pp % CORES][last].append((slot, o, pp // CORES))
    return batches, sorted(blank)


def kernel(
    nf, npan, f_hbm, q_hbm, out_ref,
    own, scaled, xbuf, ybuf, xs, ys, acc, keep, away, cxin, zout, zin, total, give, fwd, relay, direct,
    q_ref, near, local_sem, fsend, frecv, csend, crecv, zsend, zrecv, gsend, grecv, rsend, rrecv, drecv,
):
    rows, panels = own.shape
    half = panels // 2
    block = rows
    oct_rows = 8 * COMP
    octs = rows // oct_rows
    nz = npan // CORES
    f32, bf16 = jnp.float32, jnp.bfloat16

    f = lax.axis_index("freq")
    p = lax.axis_index("panel")
    z, core = p // CORES, lax.rem(p, CORES)
    odd = lax.rem(f, 2)
    mate = f + 1 - 2 * odd
    has_u = f + 2 < nf
    has_d = f >= 2
    has_x = jnp.logical_or(odd == 1, has_u)
    partner = p + 1 - 2 * core

    def dev(ff, pp):
        return {"freq": ff, "panel": pp}


    barrier = pltpu.get_barrier_semaphore()
    below, above = z > 0, z < nz - 1

    def greet(ff, pp):
        pl.semaphore_signal(barrier, inc=1, device_id=dev(ff, pp), device_id_type=MESH)

    greet(mate, p)
    greet(f, partner)

    @pl.when(below)
    def _():
        greet(f, p - CORES)

    @pl.when(above)
    def _():
        greet(f, p + CORES)

    @pl.when(has_u)
    def _():
        greet(f + 2, p)

    @pl.when(has_d)
    def _():
        greet(f - 2, p)

    loads = [
        pltpu.make_async_copy(f_hbm, own, local_sem.at[0]),
        pltpu.make_async_copy(q_hbm, q_ref, local_sem.at[1]),
    ]
    count = 2
    for there in (below, above, has_u, has_d):
        count = count + jnp.where(there, 1, 0)
    pl.semaphore_wait(barrier, count)

    def half_at(which):
        return pl.ds(pl.multiple_of(which * half, LANES), half)

    def rows_of(o, n=1):
        return pl.ds(pl.multiple_of(o * oct_rows, oct_rows), n * oct_rows)

    def field_copy(which, dst, slot, ff, step, o):
        return pltpu.make_async_remote_copy(
            src_ref=f_hbm.at[rows_of(o), half_at(which)], dst_ref=dst.at[rows_of(o), :],
            send_sem=fsend.at[slot, step], recv_sem=frecv.at[slot, step],
            device_id=dev(ff, p), device_id_type=MESH,
        )

    def to_mate(step):
        return field_copy(1 - odd, xbuf, 0, mate, step, octs - 1 - step)

    def to_lower(step):
        return field_copy(0, ybuf, 1, f - 2, step, step)

    def to_upper(step):
        return field_copy(1, ybuf, 1, f + 2, step, octs - 1 - step)

    def depart(step, carry):
        to_mate(step).start()

        @pl.when(has_d)
        def _():
            to_lower(step).start()

        @pl.when(has_u)
        def _():
            to_upper(step).start()

        return carry

    lax.fori_loop(0, octs, depart, 0)
    for load in loads:
        load.start()

    plans = [plan(role, octs, npan) for role in range(nf)]
    base = 1
    while base < 3 * octs * nz:
        base *= 2
    per = 1
    while base ** (per + 1) <= 2 ** 31:
        per += 1
    most = max(len(found) for lists, _ in plans for side in lists for found in side)
    words = max(-(-most // per), 1)

    def packed(found, w):
        value = 0
        for slot, o, zd in reversed(found[w * per:(w + 1) * per]):
            value = value * base + (slot * octs + o) * nz + zd
        return value

    def mine(seat, of):
        value = jnp.int32(0)
        for role in range(nf):
            for side in range(CORES):
                value = jnp.where(seat == role * CORES + side, jnp.int32(of(role, side)), value)
        return value

    def group(role, side, b, own_tiles):
        return [tile for tile in plans[role][0][side][b] if (tile[0] == OWN) == own_tiles]

    orders = []
    for seat in (f * CORES + 1 - core, f * CORES + core):
        for kind in (False, True):
            orders.append([
                [mine(seat, lambda role, side: len(group(role, side, b, kind)))]
                + [mine(seat, lambda role, side: packed(group(role, side, b, kind), w)) for w in range(words)]
                for b in range(octs + 1)
            ])
    LEAVE_CROSS, LEAVE_OWN, STAY_CROSS, STAY_OWN = orders
    busy = jnp.logical_or(jnp.logical_and(has_u, odd == 0), jnp.logical_and(has_d, odd == 1))

    def crossing(role, side):
        busy = (role < 2) == (role % 2 == 0)
        return [tile for tile in plans[role][0][side][octs] if busy and tile[0] == XG]

    passing = [mine(mate * CORES + core, lambda role, side: len(crossing(role, side)))]
    passing += [mine(mate * CORES + core, lambda role, side: packed(crossing(role, side), w)) for w in range(words)]

    def tell(far):
        @pl.when(jnp.logical_and(above, z >= far))
        def _():
            pl.semaphore_signal(near.at[0, far - 1], inc=1, device_id=dev(f, p + CORES), device_id_type=MESH)

        @pl.when(jnp.logical_and(below, z + far < nz))
        def _():
            pl.semaphore_signal(near.at[1, far - 1], inc=1, device_id=dev(f, p - CORES), device_id_type=MESH)

    def hear(far):
        @pl.when(z > far)
        def _():
            pl.semaphore_wait(near.at[0, far - 1], 1)

        @pl.when(z + 1 + far < nz)
        def _():
            pl.semaphore_wait(near.at[1, far - 1], 1)

    def late_bits(giver):
        value = jnp.int32(0)
        for role in range(nf):
            for pp in range(npan):
                bits = sum(2 ** o for _, o, zd in crossing(role, pp % CORES) if zd == pp // CORES)
                if bits:
                    value = jnp.where(jnp.logical_and(giver == role, p == pp), jnp.int32(bits), value)
        return value

    def is_late(bits, o):
        picked = jnp.int32(0)
        for oo in range(octs):
            picked = jnp.where(o == oo, lax.rem(lax.div(bits, 2 ** oo), 2), picked)
        return picked == 1

    given = late_bits(f)
    got = late_bits(mate)
    tell(1)

    def weight_at(where):
        index = q_ref[:, where]
        w = jnp.zeros(index.shape, f32)
        for value, entry in enumerate(QUAD_TABLE):
            w = jnp.where(index == value, jnp.float32(entry), w)
        return w

    def scale(src, dst, where, start, count):
        w = weight_at(where)

        def step(i, carry):
            at = pl.ds(pl.multiple_of(start + i * 32, 32), 32)
            dst[at, :] = (src[at, :].astype(f32) * w).astype(bf16)
            return carry

        lax.fori_loop(0, count // 32, step, 0)

    def gram(left, left_at, lo, n, right, right_at, ro, m, slot, rel):
        tall = n if panels > left_at.size else min(n, 256)
        cols = pl.ds(pl.multiple_of(rel * block + ro, LANES), m)
        over = pl.ds(ro, m)

        def step(i, carry):
            at = pl.ds(pl.multiple_of(lo + i * tall, oct_rows), tall)
            acc[slot, at, cols] = lax.dot_general(
                left[at, left_at], right[over, right_at],
                (((1,), (1,)), ((), ())), preferred_element_type=f32,
            )
            return carry

        if n == tall:
            step(0, 0)
        else:
            lax.fori_loop(0, n // tall, step, 0)

    for role in range(nf):
        @pl.when(f == role)
        def _(role=role):
            for slot, tile in plans[role][1]:
                acc[slot, :, tile * LANES:(tile + 1) * LANES] = jnp.zeros((rows, LANES), f32)

    def valid(slot, o, pp):
        t = o + pp
        low, high = t >= octs - 1, t <= 2 * octs - 1
        if slot == OWN:
            return jnp.logical_or(
                t <= octs - 1,
                jnp.logical_or(
                    jnp.logical_and(odd == 0, high),
                    jnp.logical_and(has_u, t >= 2 * octs - 1),
                ),
            )
        if slot == XG:
            return jnp.logical_and(has_x, jnp.logical_and(low, high))
        upper = jnp.logical_or(t >= 2 * octs - 1, jnp.logical_and(odd == 1, low))
        return jnp.logical_and(has_d, upper)

    def core_copy(slot, o, zd):
        return pltpu.make_async_remote_copy(
            src_ref=away.at[slot, zd, rows_of(o), :], dst_ref=cxin.at[slot, zd, rows_of(o), :],
            send_sem=csend.at[slot, zd, o], recv_sem=crecv.at[slot, zd, o],
            device_id=dev(f, partner), device_id_type=MESH,
        )

    def z_copy(slot, o, zd, source):
        return pltpu.make_async_remote_copy(
            src_ref=zout.at[slot, zd, rows_of(o), :], dst_ref=zin.at[slot, source, rows_of(o), :],
            send_sem=zsend.at[slot, zd, o], recv_sem=zrecv.at[slot, source, o],
            device_id=dev(f, zd * CORES + core), device_id_type=MESH,
        )

    def band(slot, o, zd, side, put):
        lane = pl.multiple_of((o + zd * CORES + side) * LANES, LANES)
        for c in range(8):
            at = pl.ds(pl.multiple_of(o * oct_rows + c * COMP, COMP), COMP)
            if c == 7:
                value = acc[slot, at, pl.ds(pl.multiple_of(lane + LANES, LANES), LANES)]
            else:
                pair = acc[slot, at, pl.ds(lane, 2 * LANES)]
                value = pltpu.roll(pair, 2 * LANES - COMP * (c + 1), 1)[:, :LANES]
            put(at, value)

    def send(slot, o, zd, b):
        def put(at, value):
            away[slot, zd, at, :] = value.astype(bf16)

        band(slot, o, zd, 1 - core, put)
        core_copy(slot, o, zd).start()

    def hold(slot, o, zd, b):
        def put(at, value):
            keep[slot, zd, at, :] = value

        band(slot, o, zd, core, put)

    def straight(o, zd):
        return pltpu.make_async_remote_copy(
            src_ref=zout.at[XG, zd, rows_of(o), :], dst_ref=relay.at[zd, rows_of(o), :],
            send_sem=zsend.at[XG, zd, o], recv_sem=rrecv.at[zd, o],
            device_id=dev(mate, p), device_id_type=MESH,
        )

    def onward(o, zd, source):
        return pltpu.make_async_remote_copy(
            src_ref=relay.at[zd, rows_of(o), :], dst_ref=direct.at[source, rows_of(o), :],
            send_sem=rsend.at[zd, o], recv_sem=drecv.at[source, o],
            device_id=dev(f, zd * CORES + core), device_id_type=MESH,
        )

    def hand_on(slot, o, zd, b):
        straight(o, zd).wait_recv()

        @pl.when(z != zd)
        def _():
            onward(o, zd, z).start()

    def handed(slot, o, zd, b):
        @pl.when(z != zd)
        def _():
            onward(o, zd, z).wait_send()

    def join(slot, o, zd, b):
        at = rows_of(o)
        core_copy(slot, o, zd).wait_recv()
        both = keep[slot, zd, at, :] + cxin[slot, zd, at, :].astype(f32)

        away_now = jnp.logical_and(b == octs, jnp.logical_and(slot == XG, busy))

        @pl.when(jnp.logical_and(z == zd, jnp.logical_not(away_now)))
        def _():
            total[slot, at, :] = both

        @pl.when(jnp.logical_or(z != zd, away_now))
        def _():
            zout[slot, zd, at, :] = both.astype(bf16)

        @pl.when(jnp.logical_and(z != zd, jnp.logical_not(away_now)))
        def _():
            z_copy(slot, o, zd, z).start()

        @pl.when(away_now)
        def _():
            straight(o, zd).start()

    def sent(slot, o, zd, b):
        core_copy(slot, o, zd).wait_send()

    def joined(slot, o, zd, b):
        @pl.when(jnp.logical_or(z != zd, jnp.logical_and(b == octs, jnp.logical_and(slot == XG, busy))))
        def _():
            z_copy(slot, o, zd, z).wait_send()

    def walk(act, chosen, b):
        def step(k, carry):
            code = lax.rem(carry[0], base)
            carry = (lax.div(carry[0], base),) + carry[1:]
            fresh = lax.rem(k + 1, per) == 0
            carry = tuple(jnp.where(fresh, new, old) for new, old in zip(carry[1:] + carry[-1:], carry))
            act(lax.div(code, octs * nz), lax.rem(lax.div(code, nz), octs), lax.rem(code, nz), b)
            return carry

        lax.fori_loop(0, chosen[0], step, tuple(chosen[1:]))

    def each(act, order, b):
        chosen = order[0]
        for bb in range(1, octs + 1):
            chosen = [jnp.where(b == bb, new, old) for new, old in zip(order[bb], chosen)]

        walk(act, chosen, b)

    everything = pl.ds(0, panels)
    first = pl.ds(0, half)
    second = pl.ds(half, half)
    even_now, odd_now = odd == 0, odd == 1

    for load in loads:
        load.wait()
    scale(own, scaled, everything, 0, rows)
    for far in range(1, nz - 1):
        hear(far)
        if far + 1 < nz - 1:
            tell(far + 1)
    gram(scaled, everything, 0, rows, own, everything, 0, rows, OWN, 0)

    def batch(b, carry):
        step = jnp.maximum(b - 1, 0)
        down = pl.multiple_of((octs - 1 - step) * oct_rows, oct_rows)
        up = pl.multiple_of(step * oct_rows, oct_rows)

        @pl.when(b > 0)
        def _():
            to_mate(step).wait_recv()

            @pl.when(odd_now)
            def _():
                scale(xbuf, xs, second, down, oct_rows)
                gram(xs, first, down, oct_rows, own, second, 0, rows, XG, 1)

            @pl.when(has_u)
            def _():
                to_lower(step).wait_recv()

            @pl.when(jnp.logical_and(has_u, even_now))
            def _():
                scale(xbuf, xs, first, down, oct_rows)

                @pl.when(b == octs)
                def _():
                    gram(xs, first, 0, oct_rows, ybuf, first, 0, rows, XG, 1)
                    gram(xs, first, oct_rows, rows - oct_rows, ybuf, first, rows - oct_rows, oct_rows, XG, 1)

                def cross(j, carry):
                    there = pl.multiple_of((octs - 1 - j) * oct_rows, oct_rows)
                    gram(xs, first, down, oct_rows, ybuf, first, pl.multiple_of(j * oct_rows, oct_rows), oct_rows, XG, 1)
                    gram(xs, first, there, oct_rows, ybuf, first, up, oct_rows, XG, 1)
                    return carry

                lax.fori_loop(0, jnp.where(b == octs, 0, b), cross, 0)

            @pl.when(has_d)
            def _():
                to_upper(step).wait_recv()
                scale(ybuf, ys, second, down, oct_rows)

                def up_to_down(i, carry):
                    gram(ys, first, down, oct_rows, own, second, pl.multiple_of(i * oct_rows, oct_rows), oct_rows, DG, 2)
                    return carry

                lax.fori_loop(0, octs - step, up_to_down, 0)

            @pl.when(jnp.logical_and(has_d, odd_now))
            def _():
                @pl.when(b == octs)
                def _():
                    gram(ys, first, 0, oct_rows, xbuf, first, 0, rows, DG, 1)
                    gram(ys, first, oct_rows, rows - oct_rows, xbuf, first, 0, oct_rows, DG, 1)

                def cross(j, carry):
                    there = pl.multiple_of((octs - 1 - j) * oct_rows, oct_rows)
                    gram(ys, first, down, oct_rows, xbuf, first, there, oct_rows, DG, 1)
                    gram(ys, first, there, oct_rows, xbuf, first, down, oct_rows, DG, 1)
                    return carry

                lax.fori_loop(0, jnp.where(b == octs, 0, b), cross, 0)

        each(send, LEAVE_CROSS, b)

        @pl.when(b > 0)
        def _():
            @pl.when(even_now)
            def _():
                gram(scaled, first, 0, rows, xbuf, first, down, oct_rows, OWN, 1)

            @pl.when(has_u)
            def _():
                def below_up(i, carry):
                    gram(scaled, first, pl.multiple_of(i * oct_rows, oct_rows), oct_rows, ybuf, first, up, oct_rows, OWN, 2)
                    return carry

                lax.fori_loop(step, octs, below_up, 0)

        each(send, LEAVE_OWN, b)
        each(hold, STAY_CROSS, b)
        each(join, STAY_CROSS, b)
        each(hold, STAY_OWN, b)
        each(join, STAY_OWN, b)
        return carry

    lax.fori_loop(0, octs + 1, batch, 0)
    walk(hand_on, passing, octs)

    def drain(b, carry):
        for order in (LEAVE_CROSS, LEAVE_OWN):
            each(sent, order, b)
        for order in (STAY_CROSS, STAY_OWN):
            each(joined, order, b)
        return carry

    lax.fori_loop(0, octs, drain, 0)

    def forward(slot, ff, o):
        return pltpu.make_async_remote_copy(
            src_ref=give.at[slot, rows_of(o), :], dst_ref=fwd.at[slot, rows_of(o), :],
            send_sem=gsend.at[slot, o], recv_sem=grecv.at[slot, o],
            device_id=dev(ff, p), device_id_type=MESH,
        )

    def settle(slot, target):
        def step(o, carry):
            here = valid(slot, o, p)
            if slot == XG:
                here = jnp.logical_and(here, jnp.logical_not(is_late(given, o)))

            @pl.when(here)
            def _():
                value = total[slot, rows_of(o), :]
                for hop in range(1, nz):
                    source = lax.rem(z + hop, nz)
                    z_copy(slot, o, z, source).wait_recv()
                    value = value + zin[slot, source, rows_of(o), :].astype(f32)
                total[slot, rows_of(o), :] = value
                if target is not None:
                    give[slot, rows_of(o), :] = value.astype(bf16)
                    forward(slot, target, o).start()

            if target is None:
                @pl.when(jnp.logical_not(here))
                def _():
                    total[slot, rows_of(o), :] = jnp.zeros((oct_rows, LANES), f32)

            return carry

        lax.fori_loop(0, octs, step, 0)

    def settle_direct(o, carry):
        @pl.when(is_late(got, o))
        def _():
            value = total[OWN, rows_of(o), :] + relay[z, rows_of(o), :].astype(f32)
            for hop in range(1, nz):
                source = lax.rem(z + hop, nz)
                onward(o, z, source).wait_recv()
                value = value + direct[source, rows_of(o), :].astype(f32)
            total[OWN, rows_of(o), :] = value

        return carry

    settle(XG, mate)
    settle(DG, f - 2)
    settle(OWN, None)

    mate_gives = jnp.logical_or(odd == 0, f + 1 < nf)

    def take(slot, giver, comes):
        def step(o, carry):
            @pl.when(comes(o))
            def _():
                forward(slot, giver, o).wait_recv()
                total[OWN, rows_of(o), :] = total[OWN, rows_of(o), :] + fwd[slot, rows_of(o), :].astype(f32)

            return carry

        lax.fori_loop(0, octs, step, 0)

    def from_mate(o):
        t = o + p
        here = jnp.logical_and(mate_gives, jnp.logical_and(t >= octs - 1, t <= 2 * octs - 1))
        return jnp.logical_and(here, jnp.logical_not(is_late(got, o)))

    def from_upper(o):
        t = o + p
        reach = jnp.logical_or(t >= 2 * octs - 1, jnp.logical_and(odd == 1, t >= octs - 1))
        return jnp.logical_and(has_u, reach)

    take(XG, mate, from_mate)
    take(DG, f - 2, from_upper)
    lax.fori_loop(0, octs, settle_direct, 0)

    out_ref[...] = total[OWN]

    drain(octs, 0)
    walk(handed, passing, octs)

    def close(o, carry):
        to_mate(o).wait_send()

        @pl.when(has_d)
        def _():
            to_lower(o).wait_send()

        @pl.when(has_u)
        def _():
            to_upper(o).wait_send()

        @pl.when(jnp.logical_and(valid(XG, o, p), jnp.logical_not(is_late(given, o))))
        def _():
            forward(XG, mate, o).wait_send()

        @pl.when(valid(DG, o, p))
        def _():
            forward(DG, f - 2, o).wait_send()

        return carry

    lax.fori_loop(0, octs, close, 0)


def finalize(panels_total, bw_ref, sum_ref, blocks_ref):
    f32 = jnp.float32
    freqs = blocks_ref.shape[0]
    p = lax.axis_index("panel")
    eye = lax.broadcasted_iota(jnp.int32, (freqs, freqs), 0) == lax.broadcasted_iota(
        jnp.int32, (freqs, freqs), 1
    )
    width = jnp.sum(
        jnp.where(eye, jnp.broadcast_to(bw_ref[...].astype(f32), (freqs, freqs)), 0.0), 1, keepdims=True
    )
    width = jnp.broadcast_to(width, (freqs, LANES))
    norm = jnp.float32(1.0 / math.sqrt(panels_total))
    part = lax.broadcasted_iota(jnp.int32, (freqs, LANES), 1) // COMP
    for h in range(COMP // 8):
        values = [sum_ref[pl.ds(h * 8 + a, freqs, stride=COMP), :] for a in range(8)]
        for bit in (1, 2, 4):
            upper = lax.rem(part // bit, 2) == 1
            fresh = list(values)
            for i in range(8):
                if i & bit:
                    continue
                j = i | bit
                fresh[i] = jnp.where(upper, pltpu.roll(values[j], COMP * bit, 1), values[i])
                fresh[j] = jnp.where(upper, values[j], pltpu.roll(values[i], LANES - COMP * bit, 1))
            values = fresh
        for k in range(8):
            offset = (p * 8 + k + 1).astype(f32)
            live = offset <= width
            start = (k * (COMP // 8) + h) * LANES
            blocks_ref[:, start:start + LANES] = jnp.where(live, values[k] * norm, 0.0)


def fused(nf, npan, fields, quad_index, band_width):
    freqs, comp, panels = fields.shape
    rows = freqs * comp
    nz = npan // CORES
    half = panels // 2
    octs = freqs // 8
    out_cols = REACH * freqs * comp * comp // npan
    bf16, f32 = jnp.bfloat16, jnp.float32
    dma = pltpu.SemaphoreType.DMA
    vmem = pl.BlockSpec(memory_space=pltpu.VMEM)
    sums = pl.pallas_call(
        functools.partial(kernel, nf, npan),
        out_shape=jax.ShapeDtypeStruct((rows, LANES), f32),
        in_specs=[pl.BlockSpec(memory_space=pltpu.HBM)] * 2,
        out_specs=vmem,
        scratch_shapes=[
            pltpu.VMEM((rows, panels), bf16),
            pltpu.VMEM((rows, panels), bf16),
            pltpu.VMEM((rows, half), bf16),
            pltpu.VMEM((rows, half), bf16),
            pltpu.VMEM((rows, half), bf16),
            pltpu.VMEM((rows, half), bf16),
            pltpu.VMEM((3, rows, (REACH + 1) * rows), f32),
            pltpu.VMEM((3, nz, rows, LANES), f32),
            pltpu.VMEM((3, nz, rows, LANES), bf16),
            pltpu.VMEM((3, nz, rows, LANES), bf16),
            pltpu.VMEM((3, nz, rows, LANES), bf16),
            pltpu.VMEM((3, nz, rows, LANES), bf16),
            pltpu.VMEM((3, rows, LANES), f32),
            pltpu.VMEM((3, rows, LANES), bf16),
            pltpu.VMEM((3, rows, LANES), bf16),
            pltpu.VMEM((nz, rows, LANES), bf16),
            pltpu.VMEM((nz, rows, LANES), bf16),
            pltpu.VMEM((1, panels), jnp.int32),
            pltpu.SemaphoreType.REGULAR((2, max(nz - 2, 1))),
            dma((2,)),
            dma((2, octs)), dma((2, octs)),
            dma((3, nz, octs)), dma((3, nz, octs)),
            dma((3, nz, octs)), dma((3, nz, octs)),
            dma((3, octs)), dma((3, octs)),
            dma((nz, octs)), dma((nz, octs)), dma((nz, octs)),
        ],
        compiler_params=pltpu.CompilerParams(
            collective_id=0, has_side_effects=True, vmem_limit_bytes=40 * 1024 * 1024
        ),
    )(
        pltpu.with_memory_space_constraint(fields.reshape(rows, panels), pltpu.HBM),
        pltpu.with_memory_space_constraint(quad_index.reshape(1, panels), pltpu.HBM),
    )
    return pl.pallas_call(
        functools.partial(finalize, panels * npan),
        out_shape=jax.ShapeDtypeStruct((freqs, out_cols), f32),
        in_specs=[vmem, vmem],
        out_specs=vmem,
        compiler_params=pltpu.CompilerParams(vmem_limit_bytes=8 * 1024 * 1024),
    )(band_width.reshape(1, freqs), sums)


def local(nf, npan, fields, quad_index, band_width):
    freqs, comp, panels = fields.shape
    share = REACH * freqs * comp // npan
    fits = nf == 2 * REACH and npan % CORES == 0 and share == LANES and freqs % 8 == 0 and panels % (4 * LANES) == 0
    if not fits:
        return plain(fields, quad_index, band_width)
    return fused(nf, npan, fields, quad_index, band_width)


def solution(mesh):
    placed = (P("freq", None, "panel"), P("panel"), P("freq"))
    return jax.shard_map(
        functools.partial(local, mesh.shape["freq"], mesh.shape["panel"]),
        mesh=mesh, in_specs=placed, out_specs=P("freq", "panel"), check_vma=False,
    )
```
